32 devices in a mesh: ens: 2 (over y), lat: 16 (over z, x, core).
Axes of the slice: x: 2, y: 2, z: 4, core: 2. Of those that a mesh axis runs over, the one named last changes fastest.
Arguments:
- field: bfloat16 [128, 1440, 384], P(('ens', 'lat')), parts along dimension 0, may hold values from -6 to 6
- norm_gain: float32 [384], replicated, may hold values from 0.1 to 1.9
- legendre_fwd: bfloat16 [256, 256, 64], P('lat'), as said below
- legendre_inv: bfloat16 [256, 256, 64], P('lat')
- degree_gain: float32 [256, 384], replicated, may hold values from 0.5 to 2
- mix_weight: bfloat16 [2, 384, 384], replicated, may hold values from -0.21875 to 0.21875
- mlp_gain: float32 [384], replicated, may hold values from 0.1 to 1.9
- up_weight: bfloat16 [384, 768], replicated, may hold values from -0.3125 to 0.3125
- up_bias: float32 [768], replicated, may hold values from -4 to 4
- down_weight: bfloat16 [768, 384], replicated, may hold values from -0.21875 to 0.21875
Outputs:
- result: bfloat16 [128, 1440, 384], P(('ens', 'lat')), parts along dimension 0
The draws below stay inside these ranges and needn't reach their ends.
There are 2 independent parts, one for each index of `ens`. The reference program is written for one: setup_inputs(seed, part) draws one part's arguments, and reference() takes and returns one part's arrays. A program takes and returns all parts, laid end to end along the dimension named above; an argument that names none is the same for every part. Nothing has to cross between parts.
Inputs may be any that keep to these rules, and one draw needn't show every extreme that they name: legendre_inv holds orthonormal associated Legendre functions of degree l and order m (zero where l < m) at the grid's colatitudes, legendre_fwd the same times each row's quadrature weight.
All inputs are finite; a program needn't handle non-finite values.
Results may differ from the reference program's by a relative error of at most 0.009.
Values may be sent and summed in bfloat16 or wider, within the bound.
A program may use at most 64 MiB of HBM per device.

```python
import math
import jax
import jax.numpy as jnp
from jax import lax

C = 384
NLON = 1440
MLP_WIDTH = 768
MMAX = 256
LAT_DEV = 4
LMAX = 256
LATITUDE_ROWS = 64
N_LAT = 16


def legendre_tables(key):
    jitter = 0.4
    shift = jax.random.uniform(jax.random.fold_in(key, 7), (LATITUDE_ROWS,), jnp.float32)
    rows = jnp.arange(LATITUDE_ROWS, dtype=jnp.int32).astype(jnp.float32)
    colatitude_angle = math.pi * (rows + 0.5 + jitter * (shift - 0.5)) / LATITUDE_ROWS
    zval = jnp.cos(colatitude_angle)[None, :]
    sine_value = jnp.sin(colatitude_angle)[None, :]
    quadrature_weight = math.pi / LATITUDE_ROWS * sine_value
    harmonic_order = jnp.arange(MMAX, dtype=jnp.int32).astype(jnp.float32)[:, None]
    ks = jnp.arange(1, MMAX, dtype=jnp.int32).astype(jnp.float32)
    partial_logs = jnp.concatenate([jnp.zeros((1,), jnp.float32), jnp.cumsum(jnp.log((2.0 * ks - 1.0) / (2.0 * ks)))])[:, None]
    log_norm_factor = 0.5 * jnp.log((2.0 * harmonic_order + 1.0) / (4.0 * math.pi)) + 0.5 * partial_logs
    diagonal_terms = jnp.exp(log_norm_factor + harmonic_order * jnp.log(sine_value))

    def step(carry, degree):
        before, last = carry
        lval = degree.astype(jnp.float32)
        alpha = jnp.sqrt((4.0 * lval * lval - 1.0) / jnp.maximum(lval * lval - harmonic_order * harmonic_order, 1.0))
        beta = jnp.sqrt(jnp.maximum((lval - 1.0) ** 2 - harmonic_order * harmonic_order, 0.0) / jnp.maximum(4.0 * (lval - 1.0) ** 2 - 1.0, 1.0))
        recur = alpha * (zval * last - beta * before)
        value = jnp.where(lval < harmonic_order, 0.0, jnp.where(lval == harmonic_order, diagonal_terms, recur))
        return ((last, value), value)
    start = jnp.zeros((MMAX, LATITUDE_ROWS), jnp.float32)
    unused, values = lax.scan(step, (start, start), jnp.arange(LMAX, dtype=jnp.int32))
    table = jnp.transpose(values, (1, 0, 2))
    return (table, table * quadrature_weight[None, :, :])


def draw_legendre_fwd(key, part):
    return legendre_tables(key)[1].astype(jnp.bfloat16)


def draw_legendre_inv(key, part):
    return legendre_tables(key)[0].astype(jnp.bfloat16)


def shard_levels(stream_key, extent, shards, low, top_value):
    factor_of = 1.0
    for axis_at, parts in shards:
        heights = jax.random.uniform(jax.random.fold_in(jax.random.fold_in(stream_key, 6), axis_at), (parts,), jnp.float32, low / len(shards), top_value / len(shards))
        factor_of = factor_of * jnp.repeat(jnp.exp(heights), extent[axis_at] // parts).reshape((-1,) + (1,) * (len(extent) - 1 - axis_at))
    return factor_of


def gaussian(rng, extent, width, most, cuts=(), kind=jnp.bfloat16):
    values = width * jax.random.normal(rng, extent, jnp.float32)
    if cuts:
        values = values * shard_levels(rng, extent, cuts, -0.22, 0.18)
    return jnp.clip(values, -most, most).astype(kind)


def setup_inputs(seed: int = 0, part: int = 0) -> dict:
    splits = jax.random.split(jax.random.key(seed), 11)
    own_keys = jax.random.split(jax.random.fold_in(splits[10], part), 11)
    field = gaussian(own_keys[0], (LATITUDE_ROWS, NLON, C), 1.0, 6.0, ((0, 16),))
    norm_gain = jnp.clip(1.0 + 0.18 * jax.random.normal(splits[1], (C,), jnp.float32), 0.1, 1.9)
    legendre_fwd = draw_legendre_fwd(jax.random.fold_in(splits[10], 71), part)
    legendre_inv = draw_legendre_inv(jax.random.fold_in(splits[10], 71), part)
    degree_gain = jnp.clip(jnp.exp(jax.random.uniform(splits[4], (LMAX, C), jnp.float32, math.log(0.5), math.log(2.0))), 0.5, 2.0)
    mix_weight = gaussian(splits[5], (2, C, C), (2 * C) ** -0.5, 0.21875)
    mlp_gain = jnp.clip(1.0 + 0.18 * jax.random.normal(splits[6], (C,), jnp.float32), 0.1, 1.9)
    up_weight = gaussian(splits[7], (C, MLP_WIDTH), C ** -0.5, 0.3125)
    up_bias = gaussian(splits[8], (MLP_WIDTH,), 0.7, 4.0, (), jnp.float32)
    down_weight = gaussian(splits[9], (MLP_WIDTH, C), MLP_WIDTH ** -0.5, 0.21875)
    return dict(field=field, norm_gain=norm_gain, legendre_fwd=legendre_fwd, legendre_inv=legendre_inv, degree_gain=degree_gain, mix_weight=mix_weight, mlp_gain=mlp_gain, up_weight=up_weight, up_bias=up_bias, down_weight=down_weight)


def dft_tables(nlon, modes):
    lon = jnp.arange(nlon, dtype=jnp.int32)
    wave = jnp.arange(modes, dtype=jnp.int32)
    phase = (wave[:, None] * lon[None, :] % nlon).astype(jnp.float32) * (2.0 * math.pi / nlon)
    scale = 2.0 * math.pi / nlon
    forward = jnp.stack([scale * jnp.cos(phase), -scale * jnp.sin(phase)], axis=1).reshape(2 * modes, nlon)
    weight = jnp.where(wave == 0, 1.0, 2.0).astype(jnp.float32)[:, None]
    inverse = jnp.stack([weight * jnp.cos(phase), -weight * jnp.sin(phase)], axis=1).reshape(2 * modes, nlon)
    return (forward.astype(jnp.bfloat16), inverse.T.astype(jnp.bfloat16))

def layer_norm(values, gain):
    values = values.astype(jnp.float32)
    center = values - lax.optimization_barrier(jnp.mean(values, axis=-1, keepdims=True))
    spread = lax.optimization_barrier(jnp.mean(center * center, axis=-1, keepdims=True))
    return center * lax.rsqrt(spread + 1e-05) * gain

def reference(field, norm_gain, legendre_fwd, legendre_inv, degree_gain, mix_weight, mlp_gain, up_weight, up_bias, down_weight):
    forward, inverse = dft_tables(NLON, MMAX)
    blocks = field.reshape(N_LAT, LAT_DEV, NLON, C)

    def analyse(block):
        normed = layer_norm(block, norm_gain).astype(jnp.bfloat16)
        spec = jnp.einsum('nk,jkc->jnc', forward.astype(jnp.float32), normed.astype(jnp.float32))
        return spec.astype(jnp.bfloat16)
    spectrum_lon = lax.map(analyse, blocks).reshape(LATITUDE_ROWS, MMAX, 2, C)
    coeffs = jnp.einsum('mlj,jmrc->mlrc', legendre_fwd.astype(jnp.float32), spectrum_lon.astype(jnp.float32))
    scaled = (coeffs * degree_gain[None, :, None, :]).astype(jnp.bfloat16).reshape(MMAX * LMAX, 2 * C)
    block_w = jnp.concatenate([jnp.concatenate([mix_weight[0], mix_weight[1]], 1), jnp.concatenate([-mix_weight[1], mix_weight[0]], 1)], 0)
    mixed = jnp.dot(scaled, block_w, preferred_element_type=jnp.float32).astype(jnp.bfloat16).reshape(MMAX, LMAX, 2, C)
    synth_lon = jnp.einsum('mlj,mlrc->jmrc', legendre_inv.astype(jnp.float32), mixed.astype(jnp.float32)).astype(jnp.bfloat16)
    synth_blocks = synth_lon.reshape(N_LAT, LAT_DEV, 2 * MMAX, C)

    def finish(pair):
        block, synth = pair
        normed = layer_norm(block, norm_gain).astype(jnp.bfloat16)
        filtered = jnp.einsum('kn,jnc->jkc', inverse.astype(jnp.float32), synth.astype(jnp.float32))
        inner = filtered + normed.astype(jnp.float32)
        post = layer_norm(inner, mlp_gain).astype(jnp.bfloat16).reshape(LAT_DEV * NLON, C)
        hidden = jax.nn.gelu(jnp.dot(post, up_weight, preferred_element_type=jnp.float32) + up_bias).astype(jnp.bfloat16)
        out = block.reshape(LAT_DEV * NLON, C).astype(jnp.float32) + jnp.dot(hidden, down_weight, preferred_element_type=jnp.float32)
        return out.astype(jnp.bfloat16).reshape(LAT_DEV, NLON, C)
    return lax.map(finish, (blocks, synth_blocks)).reshape(LATITUDE_ROWS, NLON, C)
```

```python
import functools
import math

import jax
import jax.numpy as jnp
import numpy as np
from jax import lax
from jax.experimental import pallas as pl
from jax.experimental.pallas import tpu as pltpu
from jax.sharding import PartitionSpec as P

NLON = 1440
MMAX = 256


def dft_tables(nlon, modes):
    lon = jnp.arange(nlon, dtype=jnp.int32)
    wave = jnp.arange(modes, dtype=jnp.int32)
    phase = (wave[:, None] * lon[None, :] % nlon).astype(jnp.float32) * (2.0 * math.pi / nlon)
    scale = 2.0 * math.pi / nlon
    forward = jnp.stack([scale * jnp.cos(phase), -scale * jnp.sin(phase)], axis=1).reshape(
        2 * modes, nlon
    )
    weight = jnp.where(wave == 0, 1.0, 2.0).astype(jnp.float32)[:, None]
    inverse = jnp.stack([weight * jnp.cos(phase), -weight * jnp.sin(phase)], axis=1).reshape(
        2 * modes, nlon
    )
    return (forward.astype(jnp.bfloat16), inverse.T.astype(jnp.bfloat16))


def layer_norm(values, gain):
    values = values.astype(jnp.float32)
    center = values - jnp.mean(values, axis=-1, keepdims=True)
    spread = jnp.mean(center * center, axis=-1, keepdims=True)
    return center * lax.rsqrt(spread + 1e-05) * gain


def plain_shards(
    field,
    norm_gain,
    legendre_fwd,
    legendre_inv,
    degree_gain,
    mix_weight,
    mlp_gain,
    up_weight,
    up_bias,
    down_weight,
):
    lat_rows, nlon, chan = field.shape
    modes_here, degrees, all_lats = legendre_fwd.shape
    forward, inverse = dft_tables(NLON, MMAX)
    normed = layer_norm(field, norm_gain).astype(jnp.bfloat16)
    spectrum_lon = jnp.einsum("nk,jkc->jnc", forward, normed, preferred_element_type=jnp.float32)
    spectrum_lon = spectrum_lon.astype(jnp.bfloat16).reshape(lat_rows, MMAX, 2, chan)
    arrived = lax.all_to_all(spectrum_lon, "lat", split_axis=1, concat_axis=0, tiled=True)
    coeffs = jnp.einsum("mlj,jmrc->mlrc", legendre_fwd, arrived, preferred_element_type=jnp.float32)
    scaled = (
        (coeffs * degree_gain[None, :, None, :])
        .astype(jnp.bfloat16)
        .reshape(modes_here * degrees, 2 * chan)
    )
    block_w = jnp.concatenate(
        [
            jnp.concatenate([mix_weight[0], mix_weight[1]], 1),
            jnp.concatenate([-mix_weight[1], mix_weight[0]], 1),
        ],
        0,
    )
    mixed = (
        jnp.dot(scaled, block_w, preferred_element_type=jnp.float32)
        .astype(jnp.bfloat16)
        .reshape(modes_here, degrees, 2, chan)
    )
    synth_lon = jnp.einsum(
        "mlj,mlrc->jmrc", legendre_inv, mixed, preferred_element_type=jnp.float32
    ).astype(jnp.bfloat16)
    returned = lax.all_to_all(synth_lon, "lat", split_axis=0, concat_axis=1, tiled=True)
    rows, waves, parts, width = returned.shape
    flat = returned.reshape(rows, waves * parts, width)
    filtered = jnp.einsum("kn,jnc->jkc", inverse, flat, preferred_element_type=jnp.float32)
    inner = filtered + normed.astype(jnp.float32)
    post = layer_norm(inner, mlp_gain).astype(jnp.bfloat16).reshape(lat_rows * nlon, chan)
    hidden = jax.nn.gelu(
        jnp.dot(post, up_weight, preferred_element_type=jnp.float32) + up_bias
    ).astype(jnp.bfloat16)
    output = field.reshape(lat_rows * nlon, chan).astype(jnp.float32) + jnp.dot(
        hidden, down_weight, preferred_element_type=jnp.float32
    )
    return output.astype(jnp.bfloat16).reshape(lat_rows, nlon, chan)


CHUNKS = 2
GATE1 = 2
UNROLL_LN, UNROLL_FIN, UNROLL_MODE = 5, 5, 8
TILE = 16
BF16, F32 = jnp.bfloat16, jnp.float32


def ordered_tables(nlon, modes, owners):
    here = modes // owners
    wave = np.arange(modes).reshape(owners, here // 2, 2).transpose(2, 0, 1).reshape(-1)
    phase = (wave[:, None] * np.arange(nlon // 2)[None, :] % nlon) * (2.0 * np.pi / nlon)
    table = np.stack([np.cos(phase), -np.sin(phase)], axis=1)
    weight = np.where(wave == 0, 1.0, 2.0)[:, None, None]
    forward = (table * (2.0 * np.pi / nlon)).reshape(2 * modes, nlon // 2)
    inverse = (table * weight).reshape(2 * modes, nlon // 2)
    return (
        jnp.asarray(forward.astype(np.float32).astype(BF16)),
        jnp.asarray(np.ascontiguousarray(inverse.T).astype(np.float32).astype(BF16)),
    )


def normalize(values, gain):
    width = values.shape[-1]
    center = values - jnp.sum(values, axis=-1, keepdims=True) * (1.0 / width)
    spread = jnp.sum(center * center, axis=-1, keepdims=True) * (1.0 / width)
    return center * lax.rsqrt(spread + 1e-05) * gain


def kernel(
    n,
    step,
    norm_gain,
    mlp_gain,
    up_bias,
    field_h,
    forward_h,
    inverse_h,
    leg_fwd_h,
    leg_inv_h,
    degree_h,
    mix_h,
    up_h,
    down_h,
    result,
    field,
    normed,
    plus,
    minus,
    post,
    forward,
    inverse,
    leg_fwd,
    leg_inv,
    degree,
    mix,
    block_w,
    up,
    down,
    swap,
    sent,
    arrived,
    by_mode,
    turned_back,
    synth,
    back_front,
    back_rest,
    flat_front,
    flat_rest,
    in_sem,
    row_sem,
    fs_sem,
    fr_sem,
    bs_sem,
    br_sem,
    cs_sem,
    cr_sem,
):
    rows, nlon, chan = field.shape
    chunks = sent.shape[0]
    modes_here, lats, degrees = leg_fwd.shape
    per_chunk = modes_here // chunks
    groups = lats // TILE
    owners = TILE // rows
    me = lax.axis_index("lat")
    half = forward.shape[0] // chunks
    middle = nlon // 2
    front = rows // 2

    row_copies = [
        pltpu.make_async_copy(field_h.at[r], field.at[r], row_sem.at[r]) for r in range(rows)
    ]
    loads = [
        pltpu.make_async_copy(a, b, in_sem.at[i])
        for i, (a, b) in enumerate(
            [
                (forward_h.at[:half], forward.at[:half]),
                (forward_h.at[half:], forward.at[half:]),
                (leg_fwd_h, leg_fwd),
                (mix_h, mix),
                (degree_h, degree),
                (leg_inv_h, leg_inv),
                (inverse_h, inverse),
                (up_h, up),
                (down_h, down),
            ]
        )
    ]
    row_copies[0].start()
    loads[0].start()

    def peer(t):
        offset = n // 2 + ((t + 1) // 2) * (2 * (t % 2) - 1)
        return (me + offset) % n

    barrier = pltpu.get_barrier_semaphore()

    def greet(t, carry):
        pl.semaphore_signal(
            barrier, inc=1, device_id={"lat": peer(t)}, device_id_type=pl.DeviceIdType.MESH
        )
        return carry

    lax.fori_loop(0, n - 1, greet, 0)

    def exchange(source, target, send_sem, recv_sem):
        def one(t, carry):
            to = peer(t)
            pltpu.make_async_remote_copy(
                src_ref=source(to),
                dst_ref=target(me),
                send_sem=send_sem,
                recv_sem=recv_sem,
                device_id={"lat": to},
                device_id_type=pl.DeviceIdType.MESH,
            ).start()
            return carry

        lax.fori_loop(0, n - 1, one, 0)
        pltpu.make_async_copy(source(me), target(me), recv_sem).start()

    def gone(piece, sem):
        pltpu.make_async_copy(piece, piece, sem).wait()

    def layer(r):
        def body(t, carry):
            low = pl.ds(pl.multiple_of(t * step, TILE), step)
            high = pl.ds(pl.multiple_of(middle + t * step, TILE), step)
            first = normalize(field[r, low, :].astype(F32), norm_gain[...]).astype(BF16)
            second = normalize(field[r, high, :].astype(F32), norm_gain[...]).astype(BF16)
            normed[r, low, :] = first
            normed[r, high, :] = second
            first, second = first.astype(F32), second.astype(F32)
            plus[low, :] = (first + second).astype(BF16)
            minus[r, low, :] = (first - second).astype(BF16)
            return carry

        lax.fori_loop(0, middle // step, body, 0, unroll=UNROLL_LN)

    def spectrum(c, r):
        folded = minus[r] if c else plus[...]
        spec = jnp.dot(
            forward[c * half : (c + 1) * half, :], folded, preferred_element_type=F32
        )
        sent[c, :, r] = spec.astype(BF16).reshape(n, TILE, chan)

    for r in range(rows):
        row_copies[r].wait()
        if r == 0:
            for copy in row_copies[1:] + loads[1:]:
                copy.start()
        layer(r)
        if r == 0:
            loads[0].wait()
        spectrum(0, r)
        if r == 0:
            pl.semaphore_wait(barrier, n - 1)
        if r < front:
            exchange(
                lambda d: sent.at[0, d, r], lambda s: arrived.at[0, s, r], fs_sem.at[r], fr_sem.at[0]
            )
    rest = pl.ds(front, rows - front)
    exchange(
        lambda d: sent.at[0, d, rest], lambda s: arrived.at[0, s, rest], fs_sem.at[front], fr_sem.at[0]
    )
    for copy in loads[1:]:
        copy.wait()
    for r in range(rows):
        spectrum(1, r)
    for r in range(GATE1):
        gone(sent.at[0, pl.ds(0, n - 1), 0], fs_sem.at[r])
    exchange(lambda d: sent.at[1, d], lambda s: arrived.at[1, s], fs_sem.at[front + 1], fr_sem.at[1])

    block_w[:chan, :chan] = mix[0]
    block_w[:chan, chan:] = mix[1]
    block_w[chan:, :chan] = -mix[1]
    block_w[chan:, chan:] = mix[0]
    a = lax.broadcasted_iota(jnp.int32, swap.shape, 0)
    b = lax.broadcasted_iota(jnp.int32, swap.shape, 1)
    swap[...] = ((a // TILE == b % TILE) & (a % TILE == b // TILE)).astype(F32).astype(BF16)

    def give_front(c):
        exchange(
            lambda d: back_front.at[c, d], lambda s: flat_front.at[c, s], bs_sem.at[c], br_sem.at[c]
        )

    def give_rest(q):
        exchange(
            lambda d: back_rest.at[q, d], lambda s: flat_rest.at[q, s], cs_sem.at[q], cr_sem.at[q]
        )

    for c in range(chunks):
        pltpu.make_async_copy(arrived.at[c], arrived.at[c], fr_sem.at[c]).wait()
        for g in range(groups):
            block = arrived[c, g * owners : (g + 1) * owners].reshape(TILE * TILE, chan)
            turned = jnp.dot(swap[...], block, preferred_element_type=F32).astype(BF16)
            by_mode[:, g * TILE : (g + 1) * TILE, :] = turned.reshape(TILE, TILE, chan)

        def one_mode(i, carry):
            m = CHUNKS * i + c
            both = jnp.concatenate([by_mode[2 * i], by_mode[2 * i + 1]], axis=1)
            coeffs = lax.dot_general(
                leg_fwd[m], both, (((0,), (0,)), ((), ())), preferred_element_type=F32
            )
            parts = [coeffs[:, :chan] * degree[...], coeffs[:, chan:] * degree[...]]
            scaled = jnp.concatenate(parts, axis=1).astype(BF16)
            rows_of = jnp.dot(leg_inv[m], scaled, preferred_element_type=F32)
            turned_back[i] = rows_of.astype(BF16)
            return carry

        lax.fori_loop(0, per_chunk, one_mode, 0, unroll=UNROLL_MODE)

        def mix_modes(i, carry):
            two = turned_back[pl.ds(2 * i, 2)].reshape(2 * lats, 2 * chan)
            mixed = jnp.dot(two, block_w[...], preferred_element_type=F32).astype(BF16)
            for k in range(2):
                synth[4 * i + 2 * k] = mixed[k * lats : (k + 1) * lats, :chan]
                synth[4 * i + 2 * k + 1] = mixed[k * lats : (k + 1) * lats, chan:]
            return carry

        lax.fori_loop(0, per_chunk // 2, mix_modes, 0, unroll=UNROLL_MODE)
        for g in range(groups):
            block = synth[:, g * TILE : (g + 1) * TILE, :].reshape(TILE * TILE, chan)
            turned = jnp.dot(swap[...], block, preferred_element_type=F32).astype(BF16)
            turned = turned.reshape(owners, rows, TILE, chan)
            own = slice(g * owners, (g + 1) * owners)
            back_front[c, own] = turned[:, :front]
            for q in range(rows - front):
                back_rest[q, own, c] = turned[:, front + q]
        if c == 0:
            for r in range(GATE1, front):
                gone(sent.at[0, pl.ds(0, n - 1), 0], fs_sem.at[r])
            gone(sent.at[0, pl.ds(0, n - 1), rest], fs_sem.at[front])
            gone(sent.at[1, pl.ds(0, n - 1)], fs_sem.at[front + 1])
        give_front(c)
    for q in range(rows - front):
        if q < chunks:
            gone(flat_front.at[q], br_sem.at[q])
        give_rest(q)
    for c in range(rows - front, chunks):
        gone(flat_front.at[c], br_sem.at[c])

    def finish_row(r):
        if r >= front:
            gone(flat_rest.at[r - front], cr_sem.at[r - front])
            waves = [flat_rest.at[r - front, :, c] for c in range(chunks)]
        else:
            waves = [flat_front.at[c, :, r] for c in range(chunks)]

        def finish(t, carry):
            low = pl.ds(pl.multiple_of(t * step, TILE), step)
            high = pl.ds(pl.multiple_of(middle + t * step, TILE), step)
            even, odd = [
                jnp.dot(
                    inverse[low, c * half : (c + 1) * half],
                    waves[c][...].reshape(half, chan),
                    preferred_element_type=F32,
                )
                for c in range(chunks)
            ]
            first = even + odd + normed[r, low, :].astype(F32)
            second = even - odd + normed[r, high, :].astype(F32)
            at = pl.multiple_of(2 * t * step, TILE)
            post[pl.ds(at, step), :] = normalize(first, mlp_gain[...]).astype(BF16)
            at = pl.multiple_of(at + step, TILE)
            post[pl.ds(at, step), :] = normalize(second, mlp_gain[...]).astype(BF16)
            return carry

        def perceive(t, carry):
            low = pl.ds(pl.multiple_of(t * step, TILE), step)
            high = pl.ds(pl.multiple_of(middle + t * step, TILE), step)
            both = post[pl.ds(pl.multiple_of(2 * t * step, TILE), 2 * step), :]
            hidden = jnp.dot(both, up[...], preferred_element_type=F32) + up_bias[...]
            hidden = jax.nn.gelu(hidden).astype(BF16)
            total = jnp.dot(hidden, down[...], preferred_element_type=F32)
            result[r, low, :] = (field[r, low, :].astype(F32) + total[:step]).astype(BF16)
            result[r, high, :] = (field[r, high, :].astype(F32) + total[step:]).astype(BF16)
            return carry

        lax.fori_loop(0, middle // step, finish, 0, unroll=UNROLL_FIN)
        lax.fori_loop(0, middle // step, perceive, 0, unroll=UNROLL_FIN)

    for r in range(rows):
        finish_row(r)

    for c in range(chunks):
        gone(back_front.at[c, pl.ds(0, n - 1)], bs_sem.at[c])
    for q in range(rows - front):
        gone(back_rest.at[q, pl.ds(0, n - 1)], cs_sem.at[q])


def shards(
    n,
    field,
    norm_gain,
    legendre_fwd,
    legendre_inv,
    degree_gain,
    mix_weight,
    mlp_gain,
    up_weight,
    up_bias,
    down_weight,
):
    args = (field, norm_gain, legendre_fwd, legendre_inv, degree_gain, mix_weight)
    args = args + (mlp_gain, up_weight, up_bias, down_weight)
    rows, nlon, chan = field.shape
    modes_here, degrees, lats = legendre_fwd.shape
    if 2 * modes_here != CHUNKS * TILE or TILE % rows or lats % TILE or nlon % (2 * TILE) or rows % 2:
        return plain_shards(*args)
    forward, inverse = ordered_tables(nlon, modes_here * n, n)
    step = nlon // 10 if nlon % (10 * TILE) == 0 else nlon // 2
    any_spec = pl.BlockSpec(memory_space=pl.ANY)
    vmem = pl.BlockSpec(memory_space=pltpu.VMEM)
    dma = pltpu.SemaphoreType.DMA
    return pl.pallas_call(
        functools.partial(kernel, n, step),
        out_shape=pltpu.VMEM(field.shape, field.dtype),
        in_specs=[vmem] * 3 + [any_spec] * 9,
        out_specs=vmem,
        scratch_shapes=[
            pltpu.VMEM((rows, nlon, chan), BF16),
            pltpu.VMEM((rows, nlon, chan), BF16),
            pltpu.VMEM((nlon // 2, chan), BF16),
            pltpu.VMEM((rows, nlon // 2, chan), BF16),
            pltpu.VMEM((nlon, chan), BF16),
            pltpu.VMEM(forward.shape, BF16),
            pltpu.VMEM(inverse.shape, BF16),
            pltpu.VMEM((modes_here, lats, degrees), BF16),
            pltpu.VMEM((modes_here, lats, degrees), BF16),
            pltpu.VMEM(degree_gain.shape, F32),
            pltpu.VMEM(mix_weight.shape, BF16),
            pltpu.VMEM((2 * chan, 2 * chan), BF16),
            pltpu.VMEM(up_weight.shape, BF16),
            pltpu.VMEM(down_weight.shape, BF16),
            pltpu.VMEM((TILE * TILE, TILE * TILE), BF16),
            pltpu.VMEM((CHUNKS, n, rows, TILE, chan), BF16),
            pltpu.VMEM((CHUNKS, n, rows, TILE, chan), BF16),
            pltpu.VMEM((TILE, lats, chan), BF16),
            pltpu.VMEM((TILE // 2, lats, 2 * chan), BF16),
            pltpu.VMEM((TILE, lats, chan), BF16),
            pltpu.VMEM((CHUNKS, n, rows // 2, TILE, chan), BF16),
            pltpu.VMEM((rows - rows // 2, n, CHUNKS, TILE, chan), BF16),
            pltpu.VMEM((CHUNKS, n, rows // 2, TILE, chan), BF16),
            pltpu.VMEM((rows - rows // 2, n, CHUNKS, TILE, chan), BF16),
            dma((9,)),
            dma((rows,)),
            dma((rows // 2 + 2,)),
            dma((CHUNKS,)),
            dma((CHUNKS,)),
            dma((CHUNKS,)),
            dma((rows - rows // 2,)),
            dma((rows - rows // 2,)),
        ],
        compiler_params=pltpu.CompilerParams(
            collective_id=0, has_side_effects=True, vmem_limit_bytes=52 << 20
        ),
    )(
        norm_gain,
        mlp_gain,
        up_bias,
        field,
        forward,
        inverse,
        jnp.swapaxes(legendre_fwd, 1, 2),
        jnp.swapaxes(legendre_inv, 1, 2),
        degree_gain,
        mix_weight,
        up_weight,
        down_weight,
    )


def solution(mesh):
    return jax.shard_map(
        functools.partial(shards, mesh.shape["lat"]),
        mesh=mesh,
        in_specs=(
            P(("ens", "lat"), None, None),
            P(),
            P("lat", None, None),
            P("lat", None, None),
            P(),
            P(),
            P(),
            P(),
            P(),
            P(),
        ),
        out_specs=P(("ens", "lat"), None, None),
        check_vma=False,
    )
```

```python
import functools
import math

import jax
import jax.numpy as jnp
import numpy as np
from jax import lax
from jax.experimental import pallas as pl
from jax.experimental.pallas import tpu as pltpu
from jax.sharding import PartitionSpec as P

NLON = 1440
MMAX = 256


def dft_tables(nlon, modes):
    lon = jnp.arange(nlon, dtype=jnp.int32)
    wave = jnp.arange(modes, dtype=jnp.int32)
    phase = (wave[:, None] * lon[None, :] % nlon).astype(jnp.float32) * (2.0 * math.pi / nlon)
    scale = 2.0 * math.pi / nlon
    forward = jnp.stack([scale * jnp.cos(phase), -scale * jnp.sin(phase)], axis=1).reshape(
        2 * modes, nlon
    )
    weight = jnp.where(wave == 0, 1.0, 2.0).astype(jnp.float32)[:, None]
    inverse = jnp.stack([weight * jnp.cos(phase), -weight * jnp.sin(phase)], axis=1).reshape(
        2 * modes, nlon
    )
    return (forward.astype(jnp.bfloat16), inverse.T.astype(jnp.bfloat16))


def layer_norm(values, gain):
    values = values.astype(jnp.float32)
    center = values - jnp.mean(values, axis=-1, keepdims=True)
    spread = jnp.mean(center * center, axis=-1, keepdims=True)
    return center * lax.rsqrt(spread + 1e-05) * gain


def plain_shards(
    field,
    norm_gain,
    legendre_fwd,
    legendre_inv,
    degree_gain,
    mix_weight,
    mlp_gain,
    up_weight,
    up_bias,
    down_weight,
):
    lat_rows, nlon, chan = field.shape
    modes_here, degrees, all_lats = legendre_fwd.shape
    forward, inverse = dft_tables(NLON, MMAX)
    normed = layer_norm(field, norm_gain).astype(jnp.bfloat16)
    spectrum_lon = jnp.einsum("nk,jkc->jnc", forward, normed, preferred_element_type=jnp.float32)
    spectrum_lon = spectrum_lon.astype(jnp.bfloat16).reshape(lat_rows, MMAX, 2, chan)
    arrived = lax.all_to_all(spectrum_lon, "lat", split_axis=1, concat_axis=0, tiled=True)
    coeffs = jnp.einsum("mlj,jmrc->mlrc", legendre_fwd, arrived, preferred_element_type=jnp.float32)
    scaled = (
        (coeffs * degree_gain[None, :, None, :])
        .astype(jnp.bfloat16)
        .reshape(modes_here * degrees, 2 * chan)
    )
    block_w = jnp.concatenate(
        [
            jnp.concatenate([mix_weight[0], mix_weight[1]], 1),
            jnp.concatenate([-mix_weight[1], mix_weight[0]], 1),
        ],
        0,
    )
    mixed = (
        jnp.dot(scaled, block_w, preferred_element_type=jnp.float32)
        .astype(jnp.bfloat16)
        .reshape(modes_here, degrees, 2, chan)
    )
    synth_lon = jnp.einsum(
        "mlj,mlrc->jmrc", legendre_inv, mixed, preferred_element_type=jnp.float32
    ).astype(jnp.bfloat16)
    returned = lax.all_to_all(synth_lon, "lat", split_axis=0, concat_axis=1, tiled=True)
    rows, waves, parts, width = returned.shape
    flat = returned.reshape(rows, waves * parts, width)
    filtered = jnp.einsum("kn,jnc->jkc", inverse, flat, preferred_element_type=jnp.float32)
    inner = filtered + normed.astype(jnp.float32)
    post = layer_norm(inner, mlp_gain).astype(jnp.bfloat16).reshape(lat_rows * nlon, chan)
    hidden = jax.nn.gelu(
        jnp.dot(post, up_weight, preferred_element_type=jnp.float32) + up_bias
    ).astype(jnp.bfloat16)
    output = field.reshape(lat_rows * nlon, chan).astype(jnp.float32) + jnp.dot(
        hidden, down_weight, preferred_element_type=jnp.float32
    )
    return output.astype(jnp.bfloat16).reshape(lat_rows, nlon, chan)


CHUNKS = 2
GATE1 = 2
UNROLL_LN, UNROLL_FIN, UNROLL_MODE = 5, 5, 8
TILE = 16
BF16, F32 = jnp.bfloat16, jnp.float32


def ordered_tables(nlon, modes, owners):
    here = modes // owners
    wave = np.arange(modes).reshape(owners, here // 2, 2).transpose(2, 0, 1).reshape(-1)
    phase = (wave[:, None] * np.arange(nlon // 2)[None, :] % nlon) * (2.0 * np.pi / nlon)
    table = np.stack([np.cos(phase), -np.sin(phase)], axis=1)
    weight = np.where(wave == 0, 1.0, 2.0)[:, None, None]
    forward = (table * (2.0 * np.pi / nlon)).reshape(2 * modes, nlon // 2)
    inverse = (table * weight).reshape(2 * modes, nlon // 2)
    return (
        jnp.asarray(forward.astype(np.float32).astype(BF16)),
        jnp.asarray(np.ascontiguousarray(inverse.T).astype(np.float32).astype(BF16)),
    )


def normalize(values, gain):
    width = values.shape[-1]
    center = values - jnp.sum(values, axis=-1, keepdims=True) * (1.0 / width)
    spread = jnp.sum(center * center, axis=-1, keepdims=True) * (1.0 / width)
    return center * lax.rsqrt(spread + 1e-05) * gain


def finish(step, waves, normed, field, write, inverse, mlp_gain, up, up_bias, down, post):
    nlon, chan = field.shape
    middle = nlon // 2
    half = inverse.shape[1] // len(waves)

    def spans(t):
        low = pl.ds(pl.multiple_of(t * step, TILE), step)
        high = pl.ds(pl.multiple_of(middle + t * step, TILE), step)
        both = pl.ds(pl.multiple_of(2 * t * step, TILE), 2 * step)
        return low, high, both

    def synthesize(t, carry):
        low, high, both = spans(t)
        even, odd = [
            jnp.dot(
                inverse[low, c * half : (c + 1) * half],
                waves[c][...].reshape(half, chan),
                preferred_element_type=F32,
            )
            for c in range(len(waves))
        ]
        first = even + odd + normed[low, :].astype(F32)
        second = even - odd + normed[high, :].astype(F32)
        first = normalize(first, mlp_gain[...]).astype(BF16)
        second = normalize(second, mlp_gain[...]).astype(BF16)
        post[both, :] = jnp.concatenate([first, second], axis=0)
        return carry

    def perceive(t, carry):
        low, high, both = spans(t)
        hidden = jnp.dot(post[both, :], up[...], preferred_element_type=F32) + up_bias[...]
        hidden = jax.nn.gelu(hidden).astype(BF16)
        total = jnp.dot(hidden, down[...], preferred_element_type=F32)
        write(low, (field[low, :].astype(F32) + total[:step]).astype(BF16))
        write(high, (field[high, :].astype(F32) + total[step:]).astype(BF16))
        return carry

    lax.fori_loop(0, middle // step, synthesize, 0, unroll=UNROLL_FIN)
    lax.fori_loop(0, middle // step, perceive, 0, unroll=UNROLL_FIN)


def last_row(
    step,
    mlp_gain,
    up_bias,
    result,
    field,
    normed,
    flat,
    inverse,
    up,
    down,
    out_h,
    post,
    row,
    sem,
    row_sem,
):
    rows = out_h.shape[0]
    done = pltpu.make_async_copy(result, out_h.at[pl.ds(0, rows - 1)], sem)
    done.start()

    def copy(at):
        return pltpu.make_async_copy(row.at[at], out_h.at[rows - 1, at], row_sem)

    def write(at, values):
        row[at, :] = values
        copy(at).start()

    waves = [flat.at[:, c] for c in range(flat.shape[1])]
    finish(step, waves, normed, field, write, inverse, mlp_gain, up, up_bias, down, post)
    pltpu.make_async_copy(row, out_h.at[rows - 1], row_sem).wait()
    done.wait()


def kernel(
    n,
    step,
    norm_gain,
    mlp_gain,
    up_bias,
    field_h,
    forward_h,
    inverse_h,
    leg_fwd_h,
    leg_inv_h,
    degree_h,
    mix_h,
    up_h,
    down_h,
    result,
    field_last,
    normed_last,
    flat_last,
    inverse,
    up,
    down,
    field,
    normed,
    plus,
    minus,
    post,
    forward,
    leg_fwd,
    leg_inv,
    degree,
    mix,
    block_w,
    swap,
    sent,
    arrived,
    by_mode,
    turned_back,
    synth,
    back_front,
    back_rest,
    flat_front,
    flat_rest,
    in_sem,
    row_sem,
    fs_sem,
    fr_sem,
    bs_sem,
    br_sem,
    cs_sem,
    cr_sem,
):
    rows, nlon, chan = field_h.shape
    chunks = sent.shape[0]
    modes_here, lats, degrees = leg_fwd.shape
    per_chunk = modes_here // chunks
    groups = lats // TILE
    owners = TILE // rows
    me = lax.axis_index("lat")
    half = forward.shape[0] // chunks
    middle = nlon // 2
    front = rows // 2

    last = rows - 1

    def field_of(r):
        return field_last if r == last else field.at[r]

    def normed_of(r):
        return normed_last if r == last else normed.at[r]

    row_copies = [
        pltpu.make_async_copy(field_h.at[r], field_of(r), row_sem.at[r]) for r in range(rows)
    ]
    loads = [
        pltpu.make_async_copy(a, b, in_sem.at[i])
        for i, (a, b) in enumerate(
            [
                (forward_h.at[:half], forward.at[:half]),
                (forward_h.at[half:], forward.at[half:]),
                (leg_fwd_h, leg_fwd),
                (mix_h, mix),
                (degree_h, degree),
                (leg_inv_h, leg_inv),
                (inverse_h, inverse),
                (up_h, up),
                (down_h, down),
            ]
        )
    ]
    row_copies[0].start()
    loads[0].start()

    def peer(t):
        return (me + t + 1) % n

    barrier = pltpu.get_barrier_semaphore()

    def greet(t, carry):
        pl.semaphore_signal(
            barrier, inc=1, device_id={"lat": peer(t)}, device_id_type=pl.DeviceIdType.MESH
        )
        return carry

    lax.fori_loop(0, n - 1, greet, 0)

    def exchange(source, target, send_sem, recv_sem):
        def one(t, carry):
            to = peer(t)
            pltpu.make_async_remote_copy(
                src_ref=source(to),
                dst_ref=target(me),
                send_sem=send_sem,
                recv_sem=recv_sem,
                device_id={"lat": to},
                device_id_type=pl.DeviceIdType.MESH,
            ).start()
            return carry

        lax.fori_loop(0, n - 1, one, 0)
        pltpu.make_async_copy(source(me), target(me), recv_sem).start()

    def gone(piece, sem):
        pltpu.make_async_copy(piece, piece, sem).wait()

    def layer(r):
        values, target = field_of(r), normed_of(r)

        def body(t, carry):
            low = pl.ds(pl.multiple_of(t * step, TILE), step)
            high = pl.ds(pl.multiple_of(middle + t * step, TILE), step)
            first = normalize(values[low, :].astype(F32), norm_gain[...]).astype(BF16)
            second = normalize(values[high, :].astype(F32), norm_gain[...]).astype(BF16)
            target[low, :] = first
            target[high, :] = second
            first, second = first.astype(F32), second.astype(F32)
            plus[low, :] = (first + second).astype(BF16)
            minus[r, low, :] = (first - second).astype(BF16)
            return carry

        lax.fori_loop(0, middle // step, body, 0, unroll=UNROLL_LN)

    def spectrum(c, r):
        folded = minus[r] if c else plus[...]
        spec = jnp.dot(
            forward[c * half : (c + 1) * half, :], folded, preferred_element_type=F32
        )
        sent[c, :, r] = spec.astype(BF16).reshape(n, TILE, chan)

    for r in range(rows):
        row_copies[r].wait()
        if r == 0:
            for copy in row_copies[1:] + loads[1:]:
                copy.start()
        layer(r)
        if r == 0:
            loads[0].wait()
        spectrum(0, r)
        if r == 0:
            pl.semaphore_wait(barrier, n - 1)
        if r < front:
            exchange(
                lambda d: sent.at[0, d, r], lambda s: arrived.at[0, s, r], fs_sem.at[r], fr_sem.at[0]
            )
    rest = pl.ds(front, rows - front)
    exchange(
        lambda d: sent.at[0, d, rest], lambda s: arrived.at[0, s, rest], fs_sem.at[front], fr_sem.at[0]
    )
    for copy in loads[1:]:
        copy.wait()
    for r in range(rows):
        spectrum(1, r)
    for r in range(GATE1):
        gone(sent.at[0, pl.ds(0, n - 1), 0], fs_sem.at[r])
    exchange(lambda d: sent.at[1, d], lambda s: arrived.at[1, s], fs_sem.at[front + 1], fr_sem.at[1])

    block_w[:chan, :chan] = mix[0]
    block_w[:chan, chan:] = mix[1]
    block_w[chan:, :chan] = -mix[1]
    block_w[chan:, chan:] = mix[0]
    a = lax.broadcasted_iota(jnp.int32, swap.shape, 0)
    b = lax.broadcasted_iota(jnp.int32, swap.shape, 1)
    swap[...] = ((a // TILE == b % TILE) & (a % TILE == b // TILE)).astype(F32).astype(BF16)

    def give_front(c):
        exchange(
            lambda d: back_front.at[c, d], lambda s: flat_front.at[c, s], bs_sem.at[c], br_sem.at[c]
        )

    def rest_of(q):
        return flat_last if q == last - front else flat_rest.at[q]

    def give_rest(q):
        exchange(
            lambda d: back_rest.at[q, d],
            lambda s: rest_of(q).at[s],
            cs_sem.at[q],
            cr_sem.at[q],
        )

    for c in range(chunks):
        pltpu.make_async_copy(arrived.at[c], arrived.at[c], fr_sem.at[c]).wait()
        for g in range(groups):
            block = arrived[c, g * owners : (g + 1) * owners].reshape(TILE * TILE, chan)
            turned = jnp.dot(swap[...], block, preferred_element_type=F32).astype(BF16)
            by_mode[:, g * TILE : (g + 1) * TILE, :] = turned.reshape(TILE, TILE, chan)

        def one_mode(i, carry):
            m = CHUNKS * i + c
            both = jnp.concatenate([by_mode[2 * i], by_mode[2 * i + 1]], axis=1)
            coeffs = lax.dot_general(
                leg_fwd[m], both, (((0,), (0,)), ((), ())), preferred_element_type=F32
            )
            parts = [coeffs[:, :chan] * degree[...], coeffs[:, chan:] * degree[...]]
            scaled = jnp.concatenate(parts, axis=1).astype(BF16)
            rows_of = jnp.dot(leg_inv[m], scaled, preferred_element_type=F32)
            turned_back[i] = rows_of.astype(BF16)
            return carry

        lax.fori_loop(0, per_chunk, one_mode, 0, unroll=UNROLL_MODE)

        def mix_modes(i, carry):
            two = turned_back[pl.ds(2 * i, 2)].reshape(2 * lats, 2 * chan)
            mixed = jnp.dot(two, block_w[...], preferred_element_type=F32).astype(BF16)
            for k in range(2):
                synth[4 * i + 2 * k] = mixed[k * lats : (k + 1) * lats, :chan]
                synth[4 * i + 2 * k + 1] = mixed[k * lats : (k + 1) * lats, chan:]
            return carry

        lax.fori_loop(0, per_chunk // 2, mix_modes, 0, unroll=UNROLL_MODE)
        for g in range(groups):
            block = synth[:, g * TILE : (g + 1) * TILE, :].reshape(TILE * TILE, chan)
            turned = jnp.dot(swap[...], block, preferred_element_type=F32).astype(BF16)
            turned = turned.reshape(owners, rows, TILE, chan)
            own = slice(g * owners, (g + 1) * owners)
            back_front[c, own] = turned[:, :front]
            for q in range(rows - front):
                back_rest[q, own, c] = turned[:, front + q]
        if c == 0:
            for r in range(GATE1, front):
                gone(sent.at[0, pl.ds(0, n - 1), 0], fs_sem.at[r])
            gone(sent.at[0, pl.ds(0, n - 1), rest], fs_sem.at[front])
            gone(sent.at[1, pl.ds(0, n - 1)], fs_sem.at[front + 1])
        give_front(c)
    for q in range(rows - front):
        if q < chunks:
            gone(flat_front.at[q], br_sem.at[q])
        give_rest(q)
    for c in range(rows - front, chunks):
        gone(flat_front.at[c], br_sem.at[c])

    for r in range(last):
        if r >= front:
            gone(rest_of(r - front), cr_sem.at[r - front])
            waves = [rest_of(r - front).at[:, c] for c in range(chunks)]
        else:
            waves = [flat_front.at[c, :, r] for c in range(chunks)]
        row = result.at[r]

        def write(at, values):
            row[at, :] = values

        finish(
            step, waves, normed.at[r], field.at[r], write, inverse, mlp_gain, up, up_bias, down, post
        )
    gone(flat_last, cr_sem.at[last - front])

    for c in range(chunks):
        gone(back_front.at[c, pl.ds(0, n - 1)], bs_sem.at[c])
    for q in range(rows - front):
        gone(back_rest.at[q, pl.ds(0, n - 1)], cs_sem.at[q])


def shards(
    n,
    field,
    norm_gain,
    legendre_fwd,
    legendre_inv,
    degree_gain,
    mix_weight,
    mlp_gain,
    up_weight,
    up_bias,
    down_weight,
):
    args = (field, norm_gain, legendre_fwd, legendre_inv, degree_gain, mix_weight)
    args = args + (mlp_gain, up_weight, up_bias, down_weight)
    rows, nlon, chan = field.shape
    modes_here, degrees, lats = legendre_fwd.shape
    if 2 * modes_here != CHUNKS * TILE or TILE % rows or lats % TILE or nlon % (2 * TILE) or rows % 2 or rows < 4:
        return plain_shards(*args)
    forward, inverse = ordered_tables(nlon, modes_here * n, n)
    step = nlon // 10 if nlon % (10 * TILE) == 0 else nlon // 2
    any_spec = pl.BlockSpec(memory_space=pl.ANY)
    vmem = pl.BlockSpec(memory_space=pltpu.VMEM)
    dma = pltpu.SemaphoreType.DMA
    low = pltpu.VMEM
    parts = pl.pallas_call(
        functools.partial(kernel, n, step),
        out_shape=(
            low((rows - 1, nlon, chan), BF16),
            low((nlon, chan), BF16),
            low((nlon, chan), BF16),
            low((n, CHUNKS, TILE, chan), BF16),
            low(inverse.shape, BF16),
            low(up_weight.shape, BF16),
            low(down_weight.shape, BF16),
        ),
        in_specs=[vmem] * 3 + [any_spec] * 9,
        out_specs=(vmem,) * 7,
        scratch_shapes=[
            low((rows - 1, nlon, chan), BF16),
            low((rows - 1, nlon, chan), BF16),
            low((nlon // 2, chan), BF16),
            low((rows, nlon // 2, chan), BF16),
            low((nlon, chan), BF16),
            low(forward.shape, BF16),
            low((modes_here, lats, degrees), BF16),
            low((modes_here, lats, degrees), BF16),
            low(degree_gain.shape, F32),
            low(mix_weight.shape, BF16),
            low((2 * chan, 2 * chan), BF16),
            low((TILE * TILE, TILE * TILE), BF16),
            low((CHUNKS, n, rows, TILE, chan), BF16),
            low((CHUNKS, n, rows, TILE, chan), BF16),
            low((TILE, lats, chan), BF16),
            low((TILE // 2, lats, 2 * chan), BF16),
            low((TILE, lats, chan), BF16),
            low((CHUNKS, n, rows // 2, TILE, chan), BF16),
            low((rows - rows // 2, n, CHUNKS, TILE, chan), BF16),
            low((CHUNKS, n, rows // 2, TILE, chan), BF16),
            low((rows - rows // 2 - 1, n, CHUNKS, TILE, chan), BF16),
            dma((9,)),
            dma((rows,)),
            dma((rows // 2 + 2,)),
            dma((CHUNKS,)),
            dma((CHUNKS,)),
            dma((CHUNKS,)),
            dma((rows - rows // 2,)),
            dma((rows - rows // 2,)),
        ],
        compiler_params=pltpu.CompilerParams(
            collective_id=0, has_side_effects=True, vmem_limit_bytes=48 << 20
        ),
    )(
        norm_gain,
        mlp_gain,
        up_bias,
        field,
        forward,
        inverse,
        jnp.swapaxes(legendre_fwd, 1, 2),
        jnp.swapaxes(legendre_inv, 1, 2),
        degree_gain,
        mix_weight,
        up_weight,
        down_weight,
    )
    parts = [pltpu.with_memory_space_constraint(part, pltpu.VMEM) for part in parts]
    return pl.pallas_call(
        functools.partial(last_row, step),
        out_shape=jax.ShapeDtypeStruct(field.shape, field.dtype),
        in_specs=[vmem] * 9,
        out_specs=any_spec,
        scratch_shapes=[
            low((nlon, chan), BF16),
            low((nlon, chan), BF16),
            dma,
            dma,
        ],
        compiler_params=pltpu.CompilerParams(vmem_limit_bytes=16 << 20),
    )(mlp_gain, up_bias, *parts)


def solution(mesh):
    return jax.shard_map(
        functools.partial(shards, mesh.shape["lat"]),
        mesh=mesh,
        in_specs=(
            P(("ens", "lat"), None, None),
            P(),
            P("lat", None, None),
            P("lat", None, None),
            P(),
            P(),
            P(),
            P(),
            P(),
            P(),
        ),
        out_specs=P(("ens", "lat"), None, None),
        check_vma=False,
    )
```

```python
import functools
import math

import jax
import jax.numpy as jnp
import numpy as np
from jax import lax
from jax.experimental import pallas as pl
from jax.experimental.pallas import tpu as pltpu
from jax.sharding import PartitionSpec as P

NLON = 1440
MMAX = 256


def dft_tables(nlon, modes):
    lon = jnp.arange(nlon, dtype=jnp.int32)
    wave = jnp.arange(modes, dtype=jnp.int32)
    phase = (wave[:, None] * lon[None, :] % nlon).astype(jnp.float32) * (2.0 * math.pi / nlon)
    scale = 2.0 * math.pi / nlon
    forward = jnp.stack([scale * jnp.cos(phase), -scale * jnp.sin(phase)], axis=1).reshape(
        2 * modes, nlon
    )
    weight = jnp.where(wave == 0, 1.0, 2.0).astype(jnp.float32)[:, None]
    inverse = jnp.stack([weight * jnp.cos(phase), -weight * jnp.sin(phase)], axis=1).reshape(
        2 * modes, nlon
    )
    return (forward.astype(jnp.bfloat16), inverse.T.astype(jnp.bfloat16))


def layer_norm(values, gain):
    values = values.astype(jnp.float32)
    center = values - jnp.mean(values, axis=-1, keepdims=True)
    spread = jnp.mean(center * center, axis=-1, keepdims=True)
    return center * lax.rsqrt(spread + 1e-05) * gain


def plain_shards(
    field,
    norm_gain,
    legendre_fwd,
    legendre_inv,
    degree_gain,
    mix_weight,
    mlp_gain,
    up_weight,
    up_bias,
    down_weight,
):
    lat_rows, nlon, chan = field.shape
    modes_here, degrees, all_lats = legendre_fwd.shape
    forward, inverse = dft_tables(NLON, MMAX)
    normed = layer_norm(field, norm_gain).astype(jnp.bfloat16)
    spectrum_lon = jnp.einsum("nk,jkc->jnc", forward, normed, preferred_element_type=jnp.float32)
    spectrum_lon = spectrum_lon.astype(jnp.bfloat16).reshape(lat_rows, MMAX, 2, chan)
    arrived = lax.all_to_all(spectrum_lon, "lat", split_axis=1, concat_axis=0, tiled=True)
    coeffs = jnp.einsum("mlj,jmrc->mlrc", legendre_fwd, arrived, preferred_element_type=jnp.float32)
    scaled = (
        (coeffs * degree_gain[None, :, None, :])
        .astype(jnp.bfloat16)
        .reshape(modes_here * degrees, 2 * chan)
    )
    block_w = jnp.concatenate(
        [
            jnp.concatenate([mix_weight[0], mix_weight[1]], 1),
            jnp.concatenate([-mix_weight[1], mix_weight[0]], 1),
        ],
        0,
    )
    mixed = (
        jnp.dot(scaled, block_w, preferred_element_type=jnp.float32)
        .astype(jnp.bfloat16)
        .reshape(modes_here, degrees, 2, chan)
    )
    synth_lon = jnp.einsum(
        "mlj,mlrc->jmrc", legendre_inv, mixed, preferred_element_type=jnp.float32
    ).astype(jnp.bfloat16)
    returned = lax.all_to_all(synth_lon, "lat", split_axis=0, concat_axis=1, tiled=True)
    rows, waves, parts, width = returned.shape
    flat = returned.reshape(rows, waves * parts, width)
    filtered = jnp.einsum("kn,jnc->jkc", inverse, flat, preferred_element_type=jnp.float32)
    inner = filtered + normed.astype(jnp.float32)
    post = layer_norm(inner, mlp_gain).astype(jnp.bfloat16).reshape(lat_rows * nlon, chan)
    hidden = jax.nn.gelu(
        jnp.dot(post, up_weight, preferred_element_type=jnp.float32) + up_bias
    ).astype(jnp.bfloat16)
    output = field.reshape(lat_rows * nlon, chan).astype(jnp.float32) + jnp.dot(
        hidden, down_weight, preferred_element_type=jnp.float32
    )
    return output.astype(jnp.bfloat16).reshape(lat_rows, nlon, chan)


CHUNKS = 2
GATE1 = 2
UNROLL_LN, UNROLL_FIN, UNROLL_MODE = 5, 5, 8
TILE = 16
BF16, F32 = jnp.bfloat16, jnp.float32


def ordered_tables(nlon, modes, owners):
    here = modes // owners
    wave = np.arange(modes).reshape(owners, here // 2, 2).transpose(2, 0, 1).reshape(-1)
    phase = (wave[:, None] * np.arange(nlon // 2)[None, :] % nlon) * (2.0 * np.pi / nlon)
    table = np.stack([np.cos(phase), -np.sin(phase)], axis=1)
    weight = np.where(wave == 0, 1.0, 2.0)[:, None, None]
    forward = (table * (2.0 * np.pi / nlon)).reshape(2 * modes, nlon // 2)
    inverse = (table * weight).reshape(2 * modes, nlon // 2)
    return (
        jnp.asarray(forward.astype(np.float32).astype(BF16)),
        jnp.asarray(np.ascontiguousarray(inverse.T).astype(np.float32).astype(BF16)),
    )


def normalize(values, gain):
    width = values.shape[-1]
    center = values - jnp.sum(values, axis=-1, keepdims=True) * (1.0 / width)
    spread = jnp.sum(center * center, axis=-1, keepdims=True) * (1.0 / width)
    return center * lax.rsqrt(spread + 1e-05) * gain


def finish(step, waves, normed, field, write, inverse, mlp_gain, up, up_bias, down, post):
    nlon, chan = field.shape
    middle = nlon // 2
    half = inverse.shape[1] // len(waves)

    def spans(t):
        low = pl.ds(pl.multiple_of(t * step, TILE), step)
        high = pl.ds(pl.multiple_of(middle + t * step, TILE), step)
        both = pl.ds(pl.multiple_of(2 * t * step, TILE), 2 * step)
        return low, high, both

    def synthesize(t, carry):
        low, high, both = spans(t)
        even, odd = [
            jnp.dot(
                inverse[low, c * half : (c + 1) * half],
                waves[c][...].reshape(half, chan),
                preferred_element_type=F32,
            )
            for c in range(len(waves))
        ]
        first = even + odd + normed[low, :].astype(F32)
        second = even - odd + normed[high, :].astype(F32)
        first = normalize(first, mlp_gain[...]).astype(BF16)
        second = normalize(second, mlp_gain[...]).astype(BF16)
        post[both, :] = jnp.concatenate([first, second], axis=0)
        return carry

    def perceive(t, carry):
        low, high, both = spans(t)
        hidden = jnp.dot(post[both, :], up[...], preferred_element_type=F32) + up_bias[...]
        hidden = jax.nn.gelu(hidden).astype(BF16)
        total = jnp.dot(hidden, down[...], preferred_element_type=F32)
        write(low, (field[low, :].astype(F32) + total[:step]).astype(BF16))
        write(high, (field[high, :].astype(F32) + total[step:]).astype(BF16))
        return carry

    lax.fori_loop(0, middle // step, synthesize, 0, unroll=UNROLL_FIN)
    lax.fori_loop(0, middle // step, perceive, 0, unroll=UNROLL_FIN)


def last_row(
    step,
    mlp_gain,
    up_bias,
    result,
    field,
    normed,
    flat,
    inverse,
    up,
    down,
    out_h,
    post,
    row,
    sem,
    row_sem,
):
    rows = out_h.shape[0]
    done = pltpu.make_async_copy(result, out_h.at[pl.ds(0, rows - 1)], sem)
    done.start()

    def copy(at):
        return pltpu.make_async_copy(row.at[at], out_h.at[rows - 1, at], row_sem)

    def write(at, values):
        row[at, :] = values
        copy(at).start()

    waves = [flat.at[:, c] for c in range(flat.shape[1])]
    finish(step, waves, normed, field, write, inverse, mlp_gain, up, up_bias, down, post)
    pltpu.make_async_copy(row, out_h.at[rows - 1], row_sem).wait()
    done.wait()


def kernel(
    n,
    step,
    norm_gain,
    mlp_gain,
    up_bias,
    field_h,
    forward_h,
    inverse_h,
    leg_fwd_h,
    leg_inv_h,
    degree_h,
    mix_h,
    up_h,
    down_h,
    result,
    field_last,
    normed_last,
    flat_last,
    inverse,
    up,
    down,
    field,
    normed,
    plus,
    minus,
    post,
    forward,
    leg_fwd,
    leg_inv,
    degree,
    mix,
    block_w,
    swap,
    sent,
    arrived,
    by_mode,
    turned_back,
    synth,
    back_front,
    back_rest,
    flat_front,
    flat_rest,
    tile_sem,
    in_sem,
    row_sem,
    fs_sem,
    fr_sem,
    bs_sem,
    br_sem,
    cs_sem,
    cr_sem,
):
    rows, nlon, chan = field_h.shape
    chunks = sent.shape[0]
    modes_here, lats, degrees = leg_fwd.shape
    per_chunk = modes_here // chunks
    groups = lats // TILE
    owners = TILE // rows
    me = lax.axis_index("lat")
    half = forward.shape[0] // chunks
    middle = nlon // 2
    front = rows // 2
    final = chunks - 1

    last = rows - 1

    def field_of(r):
        return field_last if r == last else field.at[r]

    def normed_of(r):
        return normed_last if r == last else normed.at[r]

    row_copies = [
        pltpu.make_async_copy(field_h.at[r], field_of(r), row_sem.at[r]) for r in range(1, rows)
    ]

    def tile_copies(t):
        copies = []
        for k in range(2):
            at = pl.ds(pl.multiple_of(k * middle + t * step, TILE), step)
            sem = tile_sem.at[2 * t + k]
            copies.append(pltpu.make_async_copy(field_h.at[0, at], field.at[0, at], sem))
        return copies

    loads = [
        pltpu.make_async_copy(a, b, in_sem.at[i])
        for i, (a, b) in enumerate(
            [
                (forward_h.at[:half], forward.at[:half]),
                (forward_h.at[half:], forward.at[half:]),
                (leg_fwd_h, leg_fwd),
                (mix_h, mix),
                (degree_h, degree),
                (leg_inv_h, leg_inv),
                (inverse_h, inverse),
                (up_h, up),
                (down_h, down),
            ]
        )
    ]
    for t in range(middle // step):
        for copy in tile_copies(t):
            copy.start()
    loads[0].start()

    def peer(t):
        return (me + t + 1) % n

    barrier = pltpu.get_barrier_semaphore()

    def greet(t, carry):
        pl.semaphore_signal(
            barrier, inc=1, device_id={"lat": peer(t)}, device_id_type=pl.DeviceIdType.MESH
        )
        return carry

    lax.fori_loop(0, n - 1, greet, 0)

    def exchange(source, target, send_sem, recv_sem):
        def one(t, carry):
            to = peer(t)
            pltpu.make_async_remote_copy(
                src_ref=source(to),
                dst_ref=target(me),
                send_sem=send_sem,
                recv_sem=recv_sem,
                device_id={"lat": to},
                device_id_type=pl.DeviceIdType.MESH,
            ).start()
            return carry

        lax.fori_loop(0, n - 1, one, 0)
        pltpu.make_async_copy(source(me), target(me), recv_sem).start()

    def gone(piece, sem):
        pltpu.make_async_copy(piece, piece, sem).wait()

    def layer(r):
        values, target = field_of(r), normed_of(r)

        def body(t, carry):
            if r == 0:
                for copy in tile_copies(t):
                    copy.wait()
            low = pl.ds(pl.multiple_of(t * step, TILE), step)
            high = pl.ds(pl.multiple_of(middle + t * step, TILE), step)
            first = normalize(values[low, :].astype(F32), norm_gain[...]).astype(BF16)
            second = normalize(values[high, :].astype(F32), norm_gain[...]).astype(BF16)
            target[low, :] = first
            target[high, :] = second
            first, second = first.astype(F32), second.astype(F32)
            plus[low, :] = (first + second).astype(BF16)
            minus[r, low, :] = (first - second).astype(BF16)
            return carry

        lax.fori_loop(0, middle // step, body, 0, unroll=UNROLL_LN)

    def spectrum(c, r):
        folded = minus[r] if c else plus[...]
        spec = jnp.dot(
            forward[c * half : (c + 1) * half, :], folded, preferred_element_type=F32
        )
        sent[c, :, r] = spec.astype(BF16).reshape(n, TILE, chan)

    for r in range(rows):
        if r == 0:
            for copy in row_copies + loads[1:]:
                copy.start()
        else:
            row_copies[r - 1].wait()
        layer(r)
        if r == 0:
            loads[0].wait()
        spectrum(0, r)
        if r == 0:
            pl.semaphore_wait(barrier, n - 1)
        if r < front:
            exchange(
                lambda d: sent.at[0, d, r], lambda s: arrived.at[0, s, r], fs_sem.at[r], fr_sem.at[0]
            )
    rest = pl.ds(front, rows - front)
    exchange(
        lambda d: sent.at[0, d, rest], lambda s: arrived.at[0, s, rest], fs_sem.at[front], fr_sem.at[0]
    )
    for copy in loads[1:]:
        copy.wait()
    for r in range(rows):
        spectrum(1, r)
    for r in range(GATE1):
        gone(sent.at[0, pl.ds(0, n - 1), 0], fs_sem.at[r])
    exchange(lambda d: sent.at[1, d], lambda s: arrived.at[1, s], fs_sem.at[front + 1], fr_sem.at[1])

    block_w[:chan, :chan] = mix[0]
    block_w[:chan, chan:] = mix[1]
    block_w[chan:, :chan] = -mix[1]
    block_w[chan:, chan:] = mix[0]
    a = lax.broadcasted_iota(jnp.int32, swap.shape, 0)
    b = lax.broadcasted_iota(jnp.int32, swap.shape, 1)
    swap[...] = ((a // TILE == b % TILE) & (a % TILE == b // TILE)).astype(F32).astype(BF16)

    def give_front(c):
        exchange(
            lambda d: back_front.at[c, d], lambda s: flat_front.at[c, s], bs_sem.at[c], br_sem.at[c]
        )

    def give_front_row(r):
        exchange(
            lambda d: back_front.at[final, d, r],
            lambda s: flat_front.at[final, s, r],
            bs_sem.at[final + r],
            br_sem.at[final + r],
        )

    def rest_of(q):
        return flat_last if q == last - front else flat_rest.at[q]

    def give_rest(q):
        exchange(
            lambda d: back_rest.at[q, d],
            lambda s: rest_of(q).at[s],
            cs_sem.at[q],
            cr_sem.at[q],
        )

    for c in range(chunks):
        pltpu.make_async_copy(arrived.at[c], arrived.at[c], fr_sem.at[c]).wait()
        for g in range(groups):
            block = arrived[c, g * owners : (g + 1) * owners].reshape(TILE * TILE, chan)
            turned = jnp.dot(swap[...], block, preferred_element_type=F32).astype(BF16)
            by_mode[:, g * TILE : (g + 1) * TILE, :] = turned.reshape(TILE, TILE, chan)

        def one_mode(i, carry):
            m = CHUNKS * i + c
            both = jnp.concatenate([by_mode[2 * i], by_mode[2 * i + 1]], axis=1)
            coeffs = lax.dot_general(
                leg_fwd[m], both, (((0,), (0,)), ((), ())), preferred_element_type=F32
            )
            parts = [coeffs[:, :chan] * degree[...], coeffs[:, chan:] * degree[...]]
            scaled = jnp.concatenate(parts, axis=1).astype(BF16)
            rows_of = jnp.dot(leg_inv[m], scaled, preferred_element_type=F32)
            turned_back[i] = rows_of.astype(BF16)
            return carry

        lax.fori_loop(0, per_chunk, one_mode, 0, unroll=UNROLL_MODE)

        def mix_modes(i, carry):
            two = turned_back[pl.ds(2 * i, 2)].reshape(2 * lats, 2 * chan)
            mixed = jnp.dot(two, block_w[...], preferred_element_type=F32).astype(BF16)
            for k in range(2):
                synth[4 * i + 2 * k] = mixed[k * lats : (k + 1) * lats, :chan]
                synth[4 * i + 2 * k + 1] = mixed[k * lats : (k + 1) * lats, chan:]
            return carry

        lax.fori_loop(0, per_chunk // 2, mix_modes, 0, unroll=UNROLL_MODE)
        for g in range(groups):
            block = synth[:, g * TILE : (g + 1) * TILE, :].reshape(TILE * TILE, chan)
            turned = jnp.dot(swap[...], block, preferred_element_type=F32).astype(BF16)
            turned = turned.reshape(owners, rows, TILE, chan)
            own = slice(g * owners, (g + 1) * owners)
            back_front[c, own] = turned[:, :front]
            for q in range(rows - front):
                back_rest[q, own, c] = turned[:, front + q]
        if c == 0:
            for r in range(GATE1, front):
                gone(sent.at[0, pl.ds(0, n - 1), 0], fs_sem.at[r])
            gone(sent.at[0, pl.ds(0, n - 1), rest], fs_sem.at[front])
            gone(sent.at[1, pl.ds(0, n - 1)], fs_sem.at[front + 1])
        if c < final:
            give_front(c)
    for r in range(front):
        give_front_row(r)

    for r in range(last):
        if r == 0:
            for c in range(final):
                gone(flat_front.at[c], br_sem.at[c])
        if r < front:
            gone(flat_front.at[final, :, r], br_sem.at[final + r])
            give_rest(r)
            waves = [flat_front.at[c, :, r] for c in range(chunks)]
        else:
            gone(rest_of(r - front), cr_sem.at[r - front])
            waves = [rest_of(r - front).at[:, c] for c in range(chunks)]
        row = result.at[r]

        def write(at, values):
            row[at, :] = values

        finish(
            step, waves, normed.at[r], field.at[r], write, inverse, mlp_gain, up, up_bias, down, post
        )
    gone(flat_last, cr_sem.at[last - front])

    for c in range(final):
        gone(back_front.at[c, pl.ds(0, n - 1)], bs_sem.at[c])
    for r in range(front):
        gone(back_front.at[final, pl.ds(0, n - 1), r], bs_sem.at[final + r])
    for q in range(rows - front):
        gone(back_rest.at[q, pl.ds(0, n - 1)], cs_sem.at[q])


def shards(
    n,
    field,
    norm_gain,
    legendre_fwd,
    legendre_inv,
    degree_gain,
    mix_weight,
    mlp_gain,
    up_weight,
    up_bias,
    down_weight,
):
    args = (field, norm_gain, legendre_fwd, legendre_inv, degree_gain, mix_weight)
    args = args + (mlp_gain, up_weight, up_bias, down_weight)
    rows, nlon, chan = field.shape
    modes_here, degrees, lats = legendre_fwd.shape
    if 2 * modes_here != CHUNKS * TILE or TILE % rows or lats % TILE or nlon % (2 * TILE) or rows % 2 or rows < 4:
        return plain_shards(*args)
    forward, inverse = ordered_tables(nlon, modes_here * n, n)
    step = nlon // 10 if nlon % (10 * TILE) == 0 else nlon // 2
    any_spec = pl.BlockSpec(memory_space=pl.ANY)
    vmem = pl.BlockSpec(memory_space=pltpu.VMEM)
    dma = pltpu.SemaphoreType.DMA
    low = pltpu.VMEM
    parts = pl.pallas_call(
        functools.partial(kernel, n, step),
        out_shape=(
            low((rows - 1, nlon, chan), BF16),
            low((nlon, chan), BF16),
            low((nlon, chan), BF16),
            low((n, CHUNKS, TILE, chan), BF16),
            low(inverse.shape, BF16),
            low(up_weight.shape, BF16),
            low(down_weight.shape, BF16),
        ),
        in_specs=[vmem] * 3 + [any_spec] * 9,
        out_specs=(vmem,) * 7,
        scratch_shapes=[
            low((rows - 1, nlon, chan), BF16),
            low((rows - 1, nlon, chan), BF16),
            low((nlon // 2, chan), BF16),
            low((rows, nlon // 2, chan), BF16),
            low((nlon, chan), BF16),
            low(forward.shape, BF16),
            low((modes_here, lats, degrees), BF16),
            low((modes_here, lats, degrees), BF16),
            low(degree_gain.shape, F32),
            low(mix_weight.shape, BF16),
            low((2 * chan, 2 * chan), BF16),
            low((TILE * TILE, TILE * TILE), BF16),
            low((CHUNKS, n, rows, TILE, chan), BF16),
            low((CHUNKS, n, rows, TILE, chan), BF16),
            low((TILE, lats, chan), BF16),
            low((TILE // 2, lats, 2 * chan), BF16),
            low((TILE, lats, chan), BF16),
            low((CHUNKS, n, rows // 2, TILE, chan), BF16),
            low((rows - rows // 2, n, CHUNKS, TILE, chan), BF16),
            low((CHUNKS, n, rows // 2, TILE, chan), BF16),
            low((rows - rows // 2 - 1, n, CHUNKS, TILE, chan), BF16),
            dma((nlon // step,)),
            dma((9,)),
            dma((rows,)),
            dma((rows // 2 + 2,)),
            dma((CHUNKS,)),
            dma((CHUNKS - 1 + rows // 2,)),
            dma((CHUNKS - 1 + rows // 2,)),
            dma((rows - rows // 2,)),
            dma((rows - rows // 2,)),
        ],
        compiler_params=pltpu.CompilerParams(
            collective_id=0, has_side_effects=True, vmem_limit_bytes=48 << 20
        ),
    )(
        norm_gain,
        mlp_gain,
        up_bias,
        field,
        forward,
        inverse,
        jnp.swapaxes(legendre_fwd, 1, 2),
        jnp.swapaxes(legendre_inv, 1, 2),
        degree_gain,
        mix_weight,
        up_weight,
        down_weight,
    )
    parts = [pltpu.with_memory_space_constraint(part, pltpu.VMEM) for part in parts]
    return pl.pallas_call(
        functools.partial(last_row, step),
        out_shape=jax.ShapeDtypeStruct(field.shape, field.dtype),
        in_specs=[vmem] * 9,
        out_specs=any_spec,
        scratch_shapes=[
            low((nlon, chan), BF16),
            low((nlon, chan), BF16),
            dma,
            dma,
        ],
        compiler_params=pltpu.CompilerParams(vmem_limit_bytes=16 << 20),
    )(mlp_gain, up_bias, *parts)


def solution(mesh):
    return jax.shard_map(
        functools.partial(shards, mesh.shape["lat"]),
        mesh=mesh,
        in_specs=(
            P(("ens", "lat"), None, None),
            P(),
            P("lat", None, None),
            P("lat", None, None),
            P(),
            P(),
            P(),
            P(),
            P(),
            P(),
        ),
        out_specs=P(("ens", "lat"), None, None),
        check_vma=False,
    )
```

```python
import functools
import math

import jax
import jax.numpy as jnp
import numpy as np
from jax import lax
from jax.experimental import pallas as pl
from jax.experimental.pallas import tpu as pltpu
from jax.sharding import PartitionSpec as P

NLON = 1440
MMAX = 256


def dft_tables(nlon, modes):
    lon = jnp.arange(nlon, dtype=jnp.int32)
    wave = jnp.arange(modes, dtype=jnp.int32)
    phase = (wave[:, None] * lon[None, :] % nlon).astype(jnp.float32) * (2.0 * math.pi / nlon)
    scale = 2.0 * math.pi / nlon
    forward = jnp.stack([scale * jnp.cos(phase), -scale * jnp.sin(phase)], axis=1).reshape(
        2 * modes, nlon
    )
    weight = jnp.where(wave == 0, 1.0, 2.0).astype(jnp.float32)[:, None]
    inverse = jnp.stack([weight * jnp.cos(phase), -weight * jnp.sin(phase)], axis=1).reshape(
        2 * modes, nlon
    )
    return (forward.astype(jnp.bfloat16), inverse.T.astype(jnp.bfloat16))


def layer_norm(values, gain):
    values = values.astype(jnp.float32)
    center = values - jnp.mean(values, axis=-1, keepdims=True)
    spread = jnp.mean(center * center, axis=-1, keepdims=True)
    return center * lax.rsqrt(spread + 1e-05) * gain


def plain_shards(
    field,
    norm_gain,
    legendre_fwd,
    legendre_inv,
    degree_gain,
    mix_weight,
    mlp_gain,
    up_weight,
    up_bias,
    down_weight,
):
    lat_rows, nlon, chan = field.shape
    modes_here, degrees, all_lats = legendre_fwd.shape
    forward, inverse = dft_tables(NLON, MMAX)
    normed = layer_norm(field, norm_gain).astype(jnp.bfloat16)
    spectrum_lon = jnp.einsum("nk,jkc->jnc", forward, normed, preferred_element_type=jnp.float32)
    spectrum_lon = spectrum_lon.astype(jnp.bfloat16).reshape(lat_rows, MMAX, 2, chan)
    arrived = lax.all_to_all(spectrum_lon, "lat", split_axis=1, concat_axis=0, tiled=True)
    coeffs = jnp.einsum("mlj,jmrc->mlrc", legendre_fwd, arrived, preferred_element_type=jnp.float32)
    scaled = (
        (coeffs * degree_gain[None, :, None, :])
        .astype(jnp.bfloat16)
        .reshape(modes_here * degrees, 2 * chan)
    )
    block_w = jnp.concatenate(
        [
            jnp.concatenate([mix_weight[0], mix_weight[1]], 1),
            jnp.concatenate([-mix_weight[1], mix_weight[0]], 1),
        ],
        0,
    )
    mixed = (
        jnp.dot(scaled, block_w, preferred_element_type=jnp.float32)
        .astype(jnp.bfloat16)
        .reshape(modes_here, degrees, 2, chan)
    )
    synth_lon = jnp.einsum(
        "mlj,mlrc->jmrc", legendre_inv, mixed, preferred_element_type=jnp.float32
    ).astype(jnp.bfloat16)
    returned = lax.all_to_all(synth_lon, "lat", split_axis=0, concat_axis=1, tiled=True)
    rows, waves, parts, width = returned.shape
    flat = returned.reshape(rows, waves * parts, width)
    filtered = jnp.einsum("kn,jnc->jkc", inverse, flat, preferred_element_type=jnp.float32)
    inner = filtered + normed.astype(jnp.float32)
    post = layer_norm(inner, mlp_gain).astype(jnp.bfloat16).reshape(lat_rows * nlon, chan)
    hidden = jax.nn.gelu(
        jnp.dot(post, up_weight, preferred_element_type=jnp.float32) + up_bias
    ).astype(jnp.bfloat16)
    output = field.reshape(lat_rows * nlon, chan).astype(jnp.float32) + jnp.dot(
        hidden, down_weight, preferred_element_type=jnp.float32
    )
    return output.astype(jnp.bfloat16).reshape(lat_rows, nlon, chan)


CHUNKS = 2
GATE1 = 2
UNROLL_LN, UNROLL_FIN, UNROLL_MODE = 5, 5, 8
TILE = 16
GELU_SCALE = math.sqrt(2.0 / math.pi)
BF16, F32 = jnp.bfloat16, jnp.float32


def ordered_tables(nlon, modes, owners):
    here = modes // owners
    wave = np.arange(modes).reshape(owners, here // 2, 2).transpose(2, 0, 1).reshape(-1)
    phase = (wave[:, None] * np.arange(nlon // 2)[None, :] % nlon) * (2.0 * np.pi / nlon)
    table = np.stack([np.cos(phase), -np.sin(phase)], axis=1)
    weight = np.where(wave == 0, 1.0, 2.0)[:, None, None]
    forward = (table * (2.0 * np.pi / nlon)).reshape(2 * modes, nlon // 2)
    inverse = (table * weight).reshape(2 * modes, nlon // 2)
    return (
        jnp.asarray(forward.astype(np.float32).astype(BF16)),
        jnp.asarray(np.ascontiguousarray(inverse.T).astype(np.float32).astype(BF16)),
    )


def normalize(values, gain):
    width = values.shape[-1]
    center = values - jnp.sum(values, axis=-1, keepdims=True) * (1.0 / width)
    spread = jnp.sum(center * center, axis=-1, keepdims=True) * (1.0 / width)
    return center * lax.rsqrt(spread + 1e-05) * gain


def finish(step, waves, normed, field, write, inverse, mlp_gain, up, up_bias, down, post):
    nlon, chan = field.shape
    middle = nlon // 2
    half = inverse.shape[1] // len(waves)

    def spans(t):
        low = pl.ds(pl.multiple_of(t * step, TILE), step)
        high = pl.ds(pl.multiple_of(middle + t * step, TILE), step)
        both = pl.ds(pl.multiple_of(2 * t * step, TILE), 2 * step)
        return low, high, both

    def synthesize(t, carry):
        low, high, both = spans(t)
        even, odd = [
            jnp.dot(
                inverse[low, c * half : (c + 1) * half],
                waves[c][...].reshape(half, chan),
                preferred_element_type=F32,
            )
            for c in range(len(waves))
        ]
        first = even + odd + normed[low, :].astype(F32)
        second = even - odd + normed[high, :].astype(F32)
        first = normalize(first, mlp_gain[...]).astype(BF16)
        second = normalize(second, mlp_gain[...]).astype(BF16)
        post[both, :] = jnp.concatenate([first, second], axis=0)
        return carry

    def perceive(t, carry):
        low, high, both = spans(t)
        hidden = jnp.dot(post[both, :], up[...], preferred_element_type=F32) + up_bias[...]
        bent = hidden * (GELU_SCALE + GELU_SCALE * 0.044715 * (hidden * hidden))
        hidden = (hidden + hidden * jnp.tanh(bent)).astype(BF16)
        total = jnp.dot(hidden, down[...], preferred_element_type=F32)
        write(low, (field[low, :].astype(F32) + total[:step]).astype(BF16))
        write(high, (field[high, :].astype(F32) + total[step:]).astype(BF16))
        return carry

    lax.fori_loop(0, middle // step, synthesize, 0, unroll=UNROLL_FIN)
    lax.fori_loop(0, middle // step, perceive, 0, unroll=UNROLL_FIN)


def last_row(
    step,
    mlp_gain,
    up_bias,
    result,
    field,
    normed,
    flat,
    inverse,
    up,
    down,
    out_h,
    post,
    row,
    sem,
    row_sem,
):
    rows = out_h.shape[0]
    done = pltpu.make_async_copy(result, out_h.at[pl.ds(0, rows - 1)], sem)
    done.start()

    def copy(at):
        return pltpu.make_async_copy(row.at[at], out_h.at[rows - 1, at], row_sem)

    def write(at, values):
        row[at, :] = values
        copy(at).start()

    waves = [flat.at[:, c] for c in range(flat.shape[1])]
    finish(step, waves, normed, field, write, inverse, mlp_gain, up, up_bias, down, post)
    pltpu.make_async_copy(row, out_h.at[rows - 1], row_sem).wait()
    done.wait()


def kernel(
    n,
    step,
    norm_gain,
    mlp_gain,
    up_bias,
    field_h,
    forward_h,
    inverse_h,
    leg_fwd_h,
    leg_inv_h,
    degree_h,
    mix_h,
    up_h,
    down_h,
    result,
    field_last,
    normed_last,
    flat_last,
    inverse,
    up,
    down,
    field,
    normed,
    plus,
    minus,
    post,
    forward,
    leg_fwd,
    leg_inv,
    degree,
    mix,
    block_w,
    swap,
    sent,
    arrived,
    by_mode,
    turned_back,
    synth,
    back_front,
    back_rest,
    flat_front,
    flat_rest,
    tile_sem,
    in_sem,
    row_sem,
    fs_sem,
    fr_sem,
    bs_sem,
    br_sem,
    cs_sem,
    cr_sem,
):
    rows, nlon, chan = field_h.shape
    chunks = sent.shape[0]
    modes_here, lats, degrees = leg_fwd.shape
    per_chunk = modes_here // chunks
    groups = lats // TILE
    owners = TILE // rows
    me = lax.axis_index("lat")
    half = forward.shape[0] // chunks
    middle = nlon // 2
    front = rows // 2
    final = chunks - 1

    last = rows - 1

    def field_of(r):
        return field_last if r == last else field.at[r]

    def normed_of(r):
        return normed_last if r == last else normed.at[r]

    row_copies = [
        pltpu.make_async_copy(field_h.at[r], field_of(r), row_sem.at[r]) for r in range(1, rows)
    ]

    def tile_copies(t):
        copies = []
        for k in range(2):
            at = pl.ds(pl.multiple_of(k * middle + t * step, TILE), step)
            sem = tile_sem.at[2 * t + k]
            copies.append(pltpu.make_async_copy(field_h.at[0, at], field.at[0, at], sem))
        return copies

    loads = [
        pltpu.make_async_copy(a, b, in_sem.at[i])
        for i, (a, b) in enumerate(
            [
                (forward_h.at[:half], forward.at[:half]),
                (forward_h.at[half:], forward.at[half:]),
                (leg_fwd_h, leg_fwd),
                (mix_h, mix),
                (degree_h, degree),
                (leg_inv_h, leg_inv),
                (inverse_h, inverse),
                (up_h, up),
                (down_h, down),
            ]
        )
    ]
    for t in range(middle // step):
        for copy in tile_copies(t):
            copy.start()
    loads[0].start()

    def peer(t):
        return (me + t + 1) % n

    barrier = pltpu.get_barrier_semaphore()

    def greet(t, carry):
        pl.semaphore_signal(
            barrier, inc=1, device_id={"lat": peer(t)}, device_id_type=pl.DeviceIdType.MESH
        )
        return carry

    lax.fori_loop(0, n - 1, greet, 0)

    def exchange(source, target, send_sem, recv_sem):
        def one(t, carry):
            to = peer(t)
            pltpu.make_async_remote_copy(
                src_ref=source(to),
                dst_ref=target(me),
                send_sem=send_sem,
                recv_sem=recv_sem,
                device_id={"lat": to},
                device_id_type=pl.DeviceIdType.MESH,
            ).start()
            return carry

        lax.fori_loop(0, n - 1, one, 0)
        pltpu.make_async_copy(source(me), target(me), recv_sem).start()

    def gone(piece, sem):
        pltpu.make_async_copy(piece, piece, sem).wait()

    def layer(r):
        values, target = field_of(r), normed_of(r)

        def body(t, carry):
            if r == 0:
                for copy in tile_copies(t):
                    copy.wait()
            low = pl.ds(pl.multiple_of(t * step, TILE), step)
            high = pl.ds(pl.multiple_of(middle + t * step, TILE), step)
            first = normalize(values[low, :].astype(F32), norm_gain[...]).astype(BF16)
            second = normalize(values[high, :].astype(F32), norm_gain[...]).astype(BF16)
            target[low, :] = first
            target[high, :] = second
            first, second = first.astype(F32), second.astype(F32)
            plus[low, :] = (first + second).astype(BF16)
            minus[r, low, :] = (first - second).astype(BF16)
            return carry

        lax.fori_loop(0, middle // step, body, 0, unroll=UNROLL_LN)

    def spectrum(c, r):
        folded = minus[r] if c else plus[...]
        spec = jnp.dot(
            forward[c * half : (c + 1) * half, :], folded, preferred_element_type=F32
        )
        sent[c, :, r] = spec.astype(BF16).reshape(n, TILE, chan)

    for r in range(rows):
        if r == 0:
            for copy in row_copies + loads[1:]:
                copy.start()
        else:
            row_copies[r - 1].wait()
        layer(r)
        if r == 0:
            loads[0].wait()
        spectrum(0, r)
        if r == 0:
            pl.semaphore_wait(barrier, n - 1)
        if r < front:
            exchange(
                lambda d: sent.at[0, d, r], lambda s: arrived.at[0, s, r], fs_sem.at[r], fr_sem.at[0]
            )
    rest = pl.ds(front, rows - front)
    exchange(
        lambda d: sent.at[0, d, rest], lambda s: arrived.at[0, s, rest], fs_sem.at[front], fr_sem.at[0]
    )
    for copy in loads[1:]:
        copy.wait()
    for r in range(rows):
        spectrum(1, r)
    for r in range(GATE1):
        gone(sent.at[0, pl.ds(0, n - 1), 0], fs_sem.at[r])
    exchange(lambda d: sent.at[1, d], lambda s: arrived.at[1, s], fs_sem.at[front + 1], fr_sem.at[1])

    down[...] = (down[...].astype(F32) * 0.5).astype(BF16)
    block_w[:chan, :chan] = mix[0]
    block_w[:chan, chan:] = mix[1]
    block_w[chan:, :chan] = -mix[1]
    block_w[chan:, chan:] = mix[0]
    a = lax.broadcasted_iota(jnp.int32, swap.shape, 0)
    b = lax.broadcasted_iota(jnp.int32, swap.shape, 1)
    swap[...] = ((a // TILE == b % TILE) & (a % TILE == b // TILE)).astype(F32).astype(BF16)

    def give_front(c):
        exchange(
            lambda d: back_front.at[c, d], lambda s: flat_front.at[c, s], bs_sem.at[c], br_sem.at[c]
        )

    def give_front_row(r):
        exchange(
            lambda d: back_front.at[final, d, r],
            lambda s: flat_front.at[final, s, r],
            bs_sem.at[final + r],
            br_sem.at[final + r],
        )

    def rest_of(q):
        return flat_last if q == last - front else flat_rest.at[q]

    def give_rest(q):
        exchange(
            lambda d: back_rest.at[q, d],
            lambda s: rest_of(q).at[s],
            cs_sem.at[q],
            cr_sem.at[q],
        )

    for c in range(chunks):
        pltpu.make_async_copy(arrived.at[c], arrived.at[c], fr_sem.at[c]).wait()
        for g in range(groups):
            block = arrived[c, g * owners : (g + 1) * owners].reshape(TILE * TILE, chan)
            turned = jnp.dot(swap[...], block, preferred_element_type=F32).astype(BF16)
            by_mode[:, g * TILE : (g + 1) * TILE, :] = turned.reshape(TILE, TILE, chan)

        def one_mode(i, carry):
            m = CHUNKS * i + c
            both = jnp.concatenate([by_mode[2 * i], by_mode[2 * i + 1]], axis=1)
            coeffs = lax.dot_general(
                leg_fwd[m], both, (((0,), (0,)), ((), ())), preferred_element_type=F32
            )
            parts = [coeffs[:, :chan] * degree[...], coeffs[:, chan:] * degree[...]]
            scaled = jnp.concatenate(parts, axis=1).astype(BF16)
            rows_of = jnp.dot(leg_inv[m], scaled, preferred_element_type=F32)
            turned_back[i] = rows_of.astype(BF16)
            return carry

        lax.fori_loop(0, per_chunk, one_mode, 0, unroll=UNROLL_MODE)

        def mix_modes(i, carry):
            two = turned_back[pl.ds(2 * i, 2)].reshape(2 * lats, 2 * chan)
            mixed = jnp.dot(two, block_w[...], preferred_element_type=F32).astype(BF16)
            for k in range(2):
                synth[4 * i + 2 * k] = mixed[k * lats : (k + 1) * lats, :chan]
                synth[4 * i + 2 * k + 1] = mixed[k * lats : (k + 1) * lats, chan:]
            return carry

        lax.fori_loop(0, per_chunk // 2, mix_modes, 0, unroll=UNROLL_MODE)
        for g in range(groups):
            block = synth[:, g * TILE : (g + 1) * TILE, :].reshape(TILE * TILE, chan)
            turned = jnp.dot(swap[...], block, preferred_element_type=F32).astype(BF16)
            turned = turned.reshape(owners, rows, TILE, chan)
            own = slice(g * owners, (g + 1) * owners)
            back_front[c, own] = turned[:, :front]
            for q in range(rows - front):
                back_rest[q, own, c] = turned[:, front + q]
        if c == 0:
            for r in range(GATE1, front):
                gone(sent.at[0, pl.ds(0, n - 1), 0], fs_sem.at[r])
            gone(sent.at[0, pl.ds(0, n - 1), rest], fs_sem.at[front])
            gone(sent.at[1, pl.ds(0, n - 1)], fs_sem.at[front + 1])
        if c < final:
            give_front(c)
    for r in range(front):
        give_front_row(r)

    for r in range(last):
        if r == 0:
            for c in range(final):
                gone(flat_front.at[c], br_sem.at[c])
        if r < front:
            gone(flat_front.at[final, :, r], br_sem.at[final + r])
            give_rest(r)
            waves = [flat_front.at[c, :, r] for c in range(chunks)]
        else:
            gone(rest_of(r - front), cr_sem.at[r - front])
            waves = [rest_of(r - front).at[:, c] for c in range(chunks)]
        row = result.at[r]

        def write(at, values):
            row[at, :] = values

        finish(
            step, waves, normed.at[r], field.at[r], write, inverse, mlp_gain, up, up_bias, down, post
        )
    gone(flat_last, cr_sem.at[last - front])

    for c in range(final):
        gone(back_front.at[c, pl.ds(0, n - 1)], bs_sem.at[c])
    for r in range(front):
        gone(back_front.at[final, pl.ds(0, n - 1), r], bs_sem.at[final + r])
    for q in range(rows - front):
        gone(back_rest.at[q, pl.ds(0, n - 1)], cs_sem.at[q])


def shards(
    n,
    field,
    norm_gain,
    legendre_fwd,
    legendre_inv,
    degree_gain,
    mix_weight,
    mlp_gain,
    up_weight,
    up_bias,
    down_weight,
):
    args = (field, norm_gain, legendre_fwd, legendre_inv, degree_gain, mix_weight)
    args = args + (mlp_gain, up_weight, up_bias, down_weight)
    rows, nlon, chan = field.shape
    modes_here, degrees, lats = legendre_fwd.shape
    if 2 * modes_here != CHUNKS * TILE or TILE % rows or lats % TILE or nlon % (2 * TILE) or rows % 2 or rows < 4:
        return plain_shards(*args)
    forward, inverse = ordered_tables(nlon, modes_here * n, n)
    step = nlon // 10 if nlon % (10 * TILE) == 0 else nlon // 2
    any_spec = pl.BlockSpec(memory_space=pl.ANY)
    vmem = pl.BlockSpec(memory_space=pltpu.VMEM)
    dma = pltpu.SemaphoreType.DMA
    low = pltpu.VMEM
    parts = pl.pallas_call(
        functools.partial(kernel, n, step),
        out_shape=(
            low((rows - 1, nlon, chan), BF16),
            low((nlon, chan), BF16),
            low((nlon, chan), BF16),
            low((n, CHUNKS, TILE, chan), BF16),
            low(inverse.shape, BF16),
            low(up_weight.shape, BF16),
            low(down_weight.shape, BF16),
        ),
        in_specs=[vmem] * 3 + [any_spec] * 9,
        out_specs=(vmem,) * 7,
        scratch_shapes=[
            low((rows - 1, nlon, chan), BF16),
            low((rows - 1, nlon, chan), BF16),
            low((nlon // 2, chan), BF16),
            low((rows, nlon // 2, chan), BF16),
            low((nlon, chan), BF16),
            low(forward.shape, BF16),
            low((modes_here, lats, degrees), BF16),
            low((modes_here, lats, degrees), BF16),
            low(degree_gain.shape, F32),
            low(mix_weight.shape, BF16),
            low((2 * chan, 2 * chan), BF16),
            low((TILE * TILE, TILE * TILE), BF16),
            low((CHUNKS, n, rows, TILE, chan), BF16),
            low((CHUNKS, n, rows, TILE, chan), BF16),
            low((TILE, lats, chan), BF16),
            low((TILE // 2, lats, 2 * chan), BF16),
            low((TILE, lats, chan), BF16),
            low((CHUNKS, n, rows // 2, TILE, chan), BF16),
            low((rows - rows // 2, n, CHUNKS, TILE, chan), BF16),
            low((CHUNKS, n, rows // 2, TILE, chan), BF16),
            low((rows - rows // 2 - 1, n, CHUNKS, TILE, chan), BF16),
            dma((nlon // step,)),
            dma((9,)),
            dma((rows,)),
            dma((rows // 2 + 2,)),
            dma((CHUNKS,)),
            dma((CHUNKS - 1 + rows // 2,)),
            dma((CHUNKS - 1 + rows // 2,)),
            dma((rows - rows // 2,)),
            dma((rows - rows // 2,)),
        ],
        compiler_params=pltpu.CompilerParams(
            collective_id=0, has_side_effects=True, vmem_limit_bytes=48 << 20
        ),
    )(
        norm_gain,
        mlp_gain,
        up_bias,
        field,
        forward,
        inverse,
        jnp.swapaxes(legendre_fwd, 1, 2),
        jnp.swapaxes(legendre_inv, 1, 2),
        degree_gain,
        mix_weight,
        up_weight,
        down_weight,
    )
    parts = [pltpu.with_memory_space_constraint(part, pltpu.VMEM) for part in parts]
    return pl.pallas_call(
        functools.partial(last_row, step),
        out_shape=jax.ShapeDtypeStruct(field.shape, field.dtype),
        in_specs=[vmem] * 9,
        out_specs=any_spec,
        scratch_shapes=[
            low((nlon, chan), BF16),
            low((nlon, chan), BF16),
            dma,
            dma,
        ],
        compiler_params=pltpu.CompilerParams(vmem_limit_bytes=16 << 20),
    )(mlp_gain, up_bias, *parts)


def solution(mesh):
    return jax.shard_map(
        functools.partial(shards, mesh.shape["lat"]),
        mesh=mesh,
        in_specs=(
            P(("ens", "lat"), None, None),
            P(),
            P("lat", None, None),
            P("lat", None, None),
            P(),
            P(),
            P(),
            P(),
            P(),
            P(),
        ),
        out_specs=P(("ens", "lat"), None, None),
        check_vma=False,
    )
```

```python
import functools
import math

import jax
import jax.numpy as jnp
import numpy as np
from jax import lax
from jax.experimental import pallas as pl
from jax.experimental.pallas import tpu as pltpu
from jax.sharding import PartitionSpec as P

NLON = 1440
MMAX = 256


def dft_tables(nlon, modes):
    lon = jnp.arange(nlon, dtype=jnp.int32)
    wave = jnp.arange(modes, dtype=jnp.int32)
    phase = (wave[:, None] * lon[None, :] % nlon).astype(jnp.float32) * (2.0 * math.pi / nlon)
    scale = 2.0 * math.pi / nlon
    forward = jnp.stack([scale * jnp.cos(phase), -scale * jnp.sin(phase)], axis=1).reshape(
        2 * modes, nlon
    )
    weight = jnp.where(wave == 0, 1.0, 2.0).astype(jnp.float32)[:, None]
    inverse = jnp.stack([weight * jnp.cos(phase), -weight * jnp.sin(phase)], axis=1).reshape(
        2 * modes, nlon
    )
    return (forward.astype(jnp.bfloat16), inverse.T.astype(jnp.bfloat16))


def layer_norm(values, gain):
    values = values.astype(jnp.float32)
    center = values - jnp.mean(values, axis=-1, keepdims=True)
    spread = jnp.mean(center * center, axis=-1, keepdims=True)
    return center * lax.rsqrt(spread + 1e-05) * gain


def plain_shards(
    field,
    norm_gain,
    legendre_fwd,
    legendre_inv,
    degree_gain,
    mix_weight,
    mlp_gain,
    up_weight,
    up_bias,
    down_weight,
):
    lat_rows, nlon, chan = field.shape
    modes_here, degrees, all_lats = legendre_fwd.shape
    forward, inverse = dft_tables(NLON, MMAX)
    normed = layer_norm(field, norm_gain).astype(jnp.bfloat16)
    spectrum_lon = jnp.einsum("nk,jkc->jnc", forward, normed, preferred_element_type=jnp.float32)
    spectrum_lon = spectrum_lon.astype(jnp.bfloat16).reshape(lat_rows, MMAX, 2, chan)
    arrived = lax.all_to_all(spectrum_lon, "lat", split_axis=1, concat_axis=0, tiled=True)
    coeffs = jnp.einsum("mlj,jmrc->mlrc", legendre_fwd, arrived, preferred_element_type=jnp.float32)
    scaled = (
        (coeffs * degree_gain[None, :, None, :])
        .astype(jnp.bfloat16)
        .reshape(modes_here * degrees, 2 * chan)
    )
    block_w = jnp.concatenate(
        [
            jnp.concatenate([mix_weight[0], mix_weight[1]], 1),
            jnp.concatenate([-mix_weight[1], mix_weight[0]], 1),
        ],
        0,
    )
    mixed = (
        jnp.dot(scaled, block_w, preferred_element_type=jnp.float32)
        .astype(jnp.bfloat16)
        .reshape(modes_here, degrees, 2, chan)
    )
    synth_lon = jnp.einsum(
        "mlj,mlrc->jmrc", legendre_inv, mixed, preferred_element_type=jnp.float32
    ).astype(jnp.bfloat16)
    returned = lax.all_to_all(synth_lon, "lat", split_axis=0, concat_axis=1, tiled=True)
    rows, waves, parts, width = returned.shape
    flat = returned.reshape(rows, waves * parts, width)
    filtered = jnp.einsum("kn,jnc->jkc", inverse, flat, preferred_element_type=jnp.float32)
    inner = filtered + normed.astype(jnp.float32)
    post = layer_norm(inner, mlp_gain).astype(jnp.bfloat16).reshape(lat_rows * nlon, chan)
    hidden = jax.nn.gelu(
        jnp.dot(post, up_weight, preferred_element_type=jnp.float32) + up_bias
    ).astype(jnp.bfloat16)
    output = field.reshape(lat_rows * nlon, chan).astype(jnp.float32) + jnp.dot(
        hidden, down_weight, preferred_element_type=jnp.float32
    )
    return output.astype(jnp.bfloat16).reshape(lat_rows, nlon, chan)


CHUNKS = 2
GATE1 = 2
UNROLL_LN, UNROLL_FIN, UNROLL_MODE = 5, 5, 8
TILE = 16
GELU_SCALE = math.sqrt(2.0 / math.pi)
BF16, F32 = jnp.bfloat16, jnp.float32


def ordered_tables(nlon, modes, owners):
    here = modes // owners
    wave = np.arange(modes).reshape(owners, here // 2, 2).transpose(2, 0, 1).reshape(-1)
    phase = (wave[:, None] * np.arange(nlon // 2)[None, :] % nlon) * (2.0 * np.pi / nlon)
    table = np.stack([np.cos(phase), -np.sin(phase)], axis=1)
    weight = np.where(wave == 0, 1.0, 2.0)[:, None, None]
    forward = (table * (2.0 * np.pi / nlon)).reshape(2 * modes, nlon // 2)
    inverse = (table * weight).reshape(2 * modes, nlon // 2)
    return (
        jnp.asarray(forward.astype(np.float32).astype(BF16)),
        jnp.asarray(np.ascontiguousarray(inverse.T).astype(np.float32).astype(BF16)),
    )


def normalize(values, gain):
    width = values.shape[-1]
    center = values - jnp.sum(values, axis=-1, keepdims=True) * (1.0 / width)
    spread = jnp.sum(center * center, axis=-1, keepdims=True) * (1.0 / width)
    return center * lax.rsqrt(spread + 1e-05) * gain


def finish(step, waves, normed, field, write, inverse, mlp_gain, up, up_bias, down, post):
    nlon, chan = field.shape
    middle = nlon // 2
    half = inverse.shape[1] // len(waves)

    def spans(t):
        low = pl.ds(pl.multiple_of(t * step, TILE), step)
        high = pl.ds(pl.multiple_of(middle + t * step, TILE), step)
        both = pl.ds(pl.multiple_of(2 * t * step, TILE), 2 * step)
        return low, high, both

    def synthesize(t, carry):
        low, high, both = spans(t)
        even, odd = [
            jnp.dot(
                inverse[low, c * half : (c + 1) * half],
                waves[c][...].reshape(half, chan),
                preferred_element_type=F32,
            )
            for c in range(len(waves))
        ]
        first = even + odd + normed[low, :].astype(F32)
        second = even - odd + normed[high, :].astype(F32)
        first = normalize(first, mlp_gain[...]).astype(BF16)
        second = normalize(second, mlp_gain[...]).astype(BF16)
        post[both, :] = jnp.concatenate([first, second], axis=0)
        return carry

    def perceive(t, carry):
        low, high, both = spans(t)
        hidden = jnp.dot(post[both, :], up[...], preferred_element_type=F32) + up_bias[...]
        bent = hidden * (GELU_SCALE + GELU_SCALE * 0.044715 * (hidden * hidden))
        hidden = (hidden + hidden * jnp.tanh(bent)).astype(BF16)
        total = jnp.dot(hidden, down[...], preferred_element_type=F32)
        write(low, (field[low, :].astype(F32) + total[:step]).astype(BF16))
        write(high, (field[high, :].astype(F32) + total[step:]).astype(BF16))
        return carry

    lax.fori_loop(0, middle // step, synthesize, 0, unroll=UNROLL_FIN)
    lax.fori_loop(0, middle // step, perceive, 0, unroll=UNROLL_FIN)


def last_row(
    step,
    mlp_gain,
    up_bias,
    result,
    field,
    normed,
    flat,
    inverse,
    up,
    down,
    out_h,
    post,
    row,
    sem,
    row_sem,
):
    rows = out_h.shape[0]
    done = pltpu.make_async_copy(result, out_h.at[pl.ds(0, rows - 1)], sem)
    done.start()

    def copy(at):
        return pltpu.make_async_copy(row.at[at], out_h.at[rows - 1, at], row_sem)

    def write(at, values):
        row[at, :] = values
        copy(at).start()

    waves = [flat.at[:, c] for c in range(flat.shape[1])]
    finish(step, waves, normed, field, write, inverse, mlp_gain, up, up_bias, down, post)
    pltpu.make_async_copy(row, out_h.at[rows - 1], row_sem).wait()
    done.wait()


def kernel(
    n,
    step,
    norm_gain,
    mlp_gain,
    up_bias,
    field_h,
    forward_h,
    inverse_h,
    leg_fwd_h,
    leg_inv_h,
    degree_h,
    mix_h,
    up_h,
    down_h,
    result,
    field_last,
    normed_last,
    flat_last,
    inverse,
    up,
    down,
    field,
    normed,
    plus,
    minus,
    post,
    forward,
    leg_fwd,
    leg_inv,
    degree,
    mix,
    block_w,
    swap,
    sent,
    arrived,
    by_mode,
    turned_back,
    synth,
    back_front,
    back_rest,
    flat_front,
    flat_rest,
    tile_sem,
    in_sem,
    row_sem,
    fs_sem,
    fr_sem,
    bs_sem,
    br_sem,
    cs_sem,
    cr_sem,
):
    rows, nlon, chan = field_h.shape
    chunks = sent.shape[0]
    modes_here, lats, degrees = leg_fwd.shape
    per_chunk = modes_here // chunks
    groups = lats // TILE
    owners = TILE // rows
    me = lax.axis_index("lat")
    half = forward.shape[0] // chunks
    middle = nlon // 2
    front = rows // 2
    final = chunks - 1

    last = rows - 1

    def field_of(r):
        return field_last if r == last else field.at[r]

    def normed_of(r):
        return normed_last if r == last else normed.at[r]

    row_copies = [
        pltpu.make_async_copy(field_h.at[r], field_of(r), row_sem.at[r]) for r in range(1, rows)
    ]

    def tile_copies(t):
        copies = []
        for k in range(2):
            at = pl.ds(pl.multiple_of(k * middle + t * step, TILE), step)
            sem = tile_sem.at[2 * t + k]
            copies.append(pltpu.make_async_copy(field_h.at[0, at], field.at[0, at], sem))
        return copies

    loads = [
        pltpu.make_async_copy(a, b, in_sem.at[i])
        for i, (a, b) in enumerate(
            [
                (forward_h.at[:half], forward.at[:half]),
                (forward_h.at[half:], forward.at[half:]),
                (leg_fwd_h, leg_fwd),
                (mix_h, mix),
                (degree_h, degree),
                (leg_inv_h, leg_inv),
                (inverse_h, inverse),
                (up_h, up),
                (down_h, down),
            ]
        )
    ]
    for t in range(middle // step):
        for copy in tile_copies(t):
            copy.start()
    loads[0].start()

    def peer(t):
        return (me + t + 1) % n

    barrier = pltpu.get_barrier_semaphore()

    def greet(t, carry):
        pl.semaphore_signal(
            barrier, inc=1, device_id={"lat": peer(t)}, device_id_type=pl.DeviceIdType.MESH
        )
        return carry

    lax.fori_loop(0, n - 1, greet, 0)

    def exchange(source, target, send_sem, recv_sem):
        def one(t, carry):
            to = peer(t)
            pltpu.make_async_remote_copy(
                src_ref=source(to),
                dst_ref=target(me),
                send_sem=send_sem,
                recv_sem=recv_sem,
                device_id={"lat": to},
                device_id_type=pl.DeviceIdType.MESH,
            ).start()
            return carry

        lax.fori_loop(0, n - 1, one, 0)
        pltpu.make_async_copy(source(me), target(me), recv_sem).start()

    def gone(piece, sem):
        pltpu.make_async_copy(piece, piece, sem).wait()

    def layer(r):
        values, target = field_of(r), normed_of(r)

        def body(t, carry):
            if r == 0:
                for copy in tile_copies(t):
                    copy.wait()
            low = pl.ds(pl.multiple_of(t * step, TILE), step)
            high = pl.ds(pl.multiple_of(middle + t * step, TILE), step)
            first = normalize(values[low, :].astype(F32), norm_gain[...]).astype(BF16)
            second = normalize(values[high, :].astype(F32), norm_gain[...]).astype(BF16)
            target[low, :] = first
            target[high, :] = second
            first, second = first.astype(F32), second.astype(F32)
            plus[low, :] = (first + second).astype(BF16)
            minus[r, low, :] = (first - second).astype(BF16)
            return carry

        lax.fori_loop(0, middle // step, body, 0, unroll=UNROLL_LN)

    def spectrum(c, r):
        folded = minus[r] if c else plus[...]
        spec = jnp.dot(
            forward[c * half : (c + 1) * half, :], folded, preferred_element_type=F32
        )
        sent[c, :, r] = spec.astype(BF16).reshape(n, TILE, chan)

    for r in range(rows):
        if r == 0:
            for copy in row_copies + loads[1:]:
                copy.start()
        else:
            row_copies[r - 1].wait()
        layer(r)
        if r == 0:
            loads[0].wait()
        spectrum(0, r)
        if r == 0:
            pl.semaphore_wait(barrier, n - 1)
        if r < front:
            exchange(
                lambda d: sent.at[0, d, r], lambda s: arrived.at[0, s, r], fs_sem.at[r], fr_sem.at[0]
            )
    rest = pl.ds(front, rows - front)
    exchange(
        lambda d: sent.at[0, d, rest], lambda s: arrived.at[0, s, rest], fs_sem.at[front], fr_sem.at[0]
    )
    for copy in loads[1:]:
        copy.wait()
    for r in range(rows):
        spectrum(1, r)
    for r in range(GATE1):
        gone(sent.at[0, pl.ds(0, n - 1), 0], fs_sem.at[r])
    exchange(lambda d: sent.at[1, d], lambda s: arrived.at[1, s], fs_sem.at[front + 1], fr_sem.at[1])

    down[...] = (down[...].astype(F32) * 0.5).astype(BF16)
    block_w[:chan, :chan] = mix[0]
    block_w[:chan, chan:] = mix[1]
    block_w[chan:, :chan] = -mix[1]
    block_w[chan:, chan:] = mix[0]
    a = lax.broadcasted_iota(jnp.int32, swap.shape, 0)
    b = lax.broadcasted_iota(jnp.int32, swap.shape, 1)
    swap[...] = ((a // TILE == b % TILE) & (a % TILE == b // TILE)).astype(F32).astype(BF16)

    def give_front(c):
        exchange(
            lambda d: back_front.at[c, d], lambda s: flat_front.at[c, s], bs_sem.at[c], br_sem.at[c]
        )

    def give_front_row(r):
        exchange(
            lambda d: back_front.at[final, d, r],
            lambda s: flat_front.at[final, s, r],
            bs_sem.at[final + r],
            br_sem.at[final + r],
        )

    def rest_of(q):
        return flat_last if q == last - front else flat_rest.at[q]

    def give_rest(q):
        exchange(
            lambda d: back_rest.at[q, d],
            lambda s: rest_of(q).at[s],
            cs_sem.at[q],
            cr_sem.at[q],
        )

    for c in range(chunks):
        pltpu.make_async_copy(arrived.at[c], arrived.at[c], fr_sem.at[c]).wait()
        for g in range(groups):
            block = arrived[c, g * owners : (g + 1) * owners].reshape(TILE * TILE, chan)
            turned = jnp.dot(swap[...], block, preferred_element_type=F32).astype(BF16)
            by_mode[:, g * TILE : (g + 1) * TILE, :] = turned.reshape(TILE, TILE, chan)

        def one_mode(i, carry):
            m = CHUNKS * i + c
            both = jnp.concatenate([by_mode[2 * i], by_mode[2 * i + 1]], axis=1)
            coeffs = lax.dot_general(
                leg_fwd[m], both, (((0,), (0,)), ((), ())), preferred_element_type=F32
            )
            parts = [coeffs[:, :chan] * degree[...], coeffs[:, chan:] * degree[...]]
            scaled = jnp.concatenate(parts, axis=1).astype(BF16)
            rows_of = jnp.dot(leg_inv[m], scaled, preferred_element_type=F32)
            turned_back[i] = rows_of.astype(BF16)
            return carry

        lax.fori_loop(0, per_chunk, one_mode, 0, unroll=UNROLL_MODE)

        def mix_modes(i, carry):
            two = turned_back[pl.ds(2 * i, 2)].reshape(2 * lats, 2 * chan)
            mixed = jnp.dot(two, block_w[...], preferred_element_type=F32).astype(BF16)
            for k in range(2):
                synth[4 * i + 2 * k] = mixed[k * lats : (k + 1) * lats, :chan]
                synth[4 * i + 2 * k + 1] = mixed[k * lats : (k + 1) * lats, chan:]
            return carry

        lax.fori_loop(0, per_chunk // 2, mix_modes, 0, unroll=UNROLL_MODE)
        for g in range(groups):
            block = synth[:, g * TILE : (g + 1) * TILE, :].reshape(TILE * TILE, chan)
            turned = jnp.dot(swap[...], block, preferred_element_type=F32).astype(BF16)
            turned = turned.reshape(owners, rows, TILE, chan)
            own = slice(g * owners, (g + 1) * owners)
            back_front[c, own] = turned[:, :front]
            for q in range(rows - front):
                back_rest[q, own, c] = turned[:, front + q]
        if c == 0:
            for r in range(GATE1, front):
                gone(sent.at[0, pl.ds(0, n - 1), 0], fs_sem.at[r])
            gone(sent.at[0, pl.ds(0, n - 1), rest], fs_sem.at[front])
            gone(sent.at[1, pl.ds(0, n - 1)], fs_sem.at[front + 1])
        if c < final:
            give_front(c)
    for r in range(front):
        give_front_row(r)

    for r in range(last):
        if r == 0:
            for c in range(final):
                gone(flat_front.at[c], br_sem.at[c])
        if r < front:
            if r == 0:
                give_rest(0)
            gone(flat_front.at[final, :, r], br_sem.at[final + r])
            if r:
                give_rest(r)
            waves = [flat_front.at[c, :, r] for c in range(chunks)]
        else:
            gone(rest_of(r - front), cr_sem.at[r - front])
            waves = [rest_of(r - front).at[:, c] for c in range(chunks)]
        row = result.at[r]

        def write(at, values):
            row[at, :] = values

        finish(
            step, waves, normed.at[r], field.at[r], write, inverse, mlp_gain, up, up_bias, down, post
        )
    gone(flat_last, cr_sem.at[last - front])

    for c in range(final):
        gone(back_front.at[c, pl.ds(0, n - 1)], bs_sem.at[c])
    for r in range(front):
        gone(back_front.at[final, pl.ds(0, n - 1), r], bs_sem.at[final + r])
    for q in range(rows - front):
        gone(back_rest.at[q, pl.ds(0, n - 1)], cs_sem.at[q])


def shards(
    n,
    field,
    norm_gain,
    legendre_fwd,
    legendre_inv,
    degree_gain,
    mix_weight,
    mlp_gain,
    up_weight,
    up_bias,
    down_weight,
):
    args = (field, norm_gain, legendre_fwd, legendre_inv, degree_gain, mix_weight)
    args = args + (mlp_gain, up_weight, up_bias, down_weight)
    rows, nlon, chan = field.shape
    modes_here, degrees, lats = legendre_fwd.shape
    if 2 * modes_here != CHUNKS * TILE or TILE % rows or lats % TILE or nlon % (2 * TILE) or rows % 2 or rows < 4:
        return plain_shards(*args)
    forward, inverse = ordered_tables(nlon, modes_here * n, n)
    step = nlon // 10 if nlon % (10 * TILE) == 0 else nlon // 2
    any_spec = pl.BlockSpec(memory_space=pl.ANY)
    vmem = pl.BlockSpec(memory_space=pltpu.VMEM)
    dma = pltpu.SemaphoreType.DMA
    low = pltpu.VMEM
    parts = pl.pallas_call(
        functools.partial(kernel, n, step),
        out_shape=(
            low((rows - 1, nlon, chan), BF16),
            low((nlon, chan), BF16),
            low((nlon, chan), BF16),
            low((n, CHUNKS, TILE, chan), BF16),
            low(inverse.shape, BF16),
            low(up_weight.shape, BF16),
            low(down_weight.shape, BF16),
        ),
        in_specs=[vmem] * 3 + [any_spec] * 9,
        out_specs=(vmem,) * 7,
        scratch_shapes=[
            low((rows - 1, nlon, chan), BF16),
            low((rows - 1, nlon, chan), BF16),
            low((nlon // 2, chan), BF16),
            low((rows, nlon // 2, chan), BF16),
            low((nlon, chan), BF16),
            low(forward.shape, BF16),
            low((modes_here, lats, degrees), BF16),
            low((modes_here, lats, degrees), BF16),
            low(degree_gain.shape, F32),
            low(mix_weight.shape, BF16),
            low((2 * chan, 2 * chan), BF16),
            low((TILE * TILE, TILE * TILE), BF16),
            low((CHUNKS, n, rows, TILE, chan), BF16),
            low((CHUNKS, n, rows, TILE, chan), BF16),
            low((TILE, lats, chan), BF16),
            low((TILE // 2, lats, 2 * chan), BF16),
            low((TILE, lats, chan), BF16),
            low((CHUNKS, n, rows // 2, TILE, chan), BF16),
            low((rows - rows // 2, n, CHUNKS, TILE, chan), BF16),
            low((CHUNKS, n, rows // 2, TILE, chan), BF16),
            low((rows - rows // 2 - 1, n, CHUNKS, TILE, chan), BF16),
            dma((nlon // step,)),
            dma((9,)),
            dma((rows,)),
            dma((rows // 2 + 2,)),
            dma((CHUNKS,)),
            dma((CHUNKS - 1 + rows // 2,)),
            dma((CHUNKS - 1 + rows // 2,)),
            dma((rows - rows // 2,)),
            dma((rows - rows // 2,)),
        ],
        compiler_params=pltpu.CompilerParams(
            collective_id=0, has_side_effects=True, vmem_limit_bytes=48 << 20
        ),
    )(
        norm_gain,
        mlp_gain,
        up_bias,
        field,
        forward,
        inverse,
        jnp.swapaxes(legendre_fwd, 1, 2),
        jnp.swapaxes(legendre_inv, 1, 2),
        degree_gain,
        mix_weight,
        up_weight,
        down_weight,
    )
    parts = [pltpu.with_memory_space_constraint(part, pltpu.VMEM) for part in parts]
    return pl.pallas_call(
        functools.partial(last_row, step),
        out_shape=jax.ShapeDtypeStruct(field.shape, field.dtype),
        in_specs=[vmem] * 9,
        out_specs=any_spec,
        scratch_shapes=[
            low((nlon, chan), BF16),
            low((nlon, chan), BF16),
            dma,
            dma,
        ],
        compiler_params=pltpu.CompilerParams(vmem_limit_bytes=16 << 20),
    )(mlp_gain, up_bias, *parts)


def solution(mesh):
    return jax.shard_map(
        functools.partial(shards, mesh.shape["lat"]),
        mesh=mesh,
        in_specs=(
            P(("ens", "lat"), None, None),
            P(),
            P("lat", None, None),
            P("lat", None, None),
            P(),
            P(),
            P(),
            P(),
            P(),
            P(),
        ),
        out_specs=P(("ens", "lat"), None, None),
        check_vma=False,
    )
```
